32 devices in a mesh: grp: 2 (over y), blk: 4 (over z), sub: 2 (over x), pair: 2 (over core).
Axes of the slice: x: 2, y: 2, z: 4, core: 2. Of those that a mesh axis runs over, the one named last changes fastest.
Arguments:
- grad_volume: bfloat16 [16, 128, 8192], P(('grp', 'blk', 'sub'), 'pair'), parts along dimension 0, may hold values from -6 to 6
- query_feats: bfloat16 [16384, 1024], P(('grp', 'blk')), parts along dimension 0, may hold values from -6 to 6
- support_feats: bfloat16 [16, 128, 1024], P(('grp', 'blk', 'sub'), 'pair'), parts along dimension 0, may hold values from -6 to 6
- query_kernel: float32 [3, 3], replicated, may hold values from -2 to 2
- support_kernel: float32 [3, 3], replicated, may hold values from -2 to 2
Outputs:
- query_grad: float32 [16384, 1024], P(('grp', 'blk', 'sub', 'pair')), parts along dimension 0
- support_grad: float32 [16, 128, 1024], P(('grp', 'blk', 'sub'), 'pair'), parts along dimension 0
The draws below stay inside these ranges and needn't reach their ends.
There are 2 independent parts, one for each index of `grp`. The reference program is written for one: setup_inputs(seed, part) draws one part's arguments, and reference() takes and returns one part's arrays. A program takes and returns all parts, laid end to end along the dimension named above; an argument that names none is the same for every part. Nothing has to cross between parts.
All inputs are finite; a program needn't handle non-finite values.
Results may differ from the reference program's by a relative error of at most 0.0029.
Values may be sent and summed in bfloat16 or wider, within the bound.
No kernel may reach another device: no remote copies, remote signals or barrier semaphores. Data moves between devices by JAX's collectives and lax.ppermute only.
A program may use at most 64 MiB of HBM per device.

```python
import math
import jax
import jax.numpy as jnp
from jax import lax

CH = 1024
QW = 128
QH = 64
SW = 128
SH = 8
Q = 8192


def block_levels(key, shape, split, low, high):
    gain = 1.0
    for axis_at, parts in split:
        heights = jax.random.uniform(jax.random.fold_in(jax.random.fold_in(key, 6), axis_at), (parts,), jnp.float32, low / len(split), high / len(split))
        gain = gain * jnp.repeat(jnp.exp(heights), shape[axis_at] // parts).reshape((-1,) + (1,) * (len(shape) - 1 - axis_at))
    return gain


def noise(key, dims, width, bound, split=(), kind=jnp.bfloat16):
    entries = jax.random.normal(key, dims, jnp.float32) * width
    if len(split) > 0:
        entries = block_levels(key, dims, split, -0.22, 0.18) * entries
    return jnp.clip(entries, min=-bound, max=bound).astype(kind)


def setup_inputs(seed: int = 0, part: int = 0) -> dict:
    arg_keys = jax.random.split(jax.random.key(seed), 6)
    part_keys = jax.random.split(jax.random.fold_in(arg_keys[5], part), 6)
    grad_volume = noise(part_keys[0], (SH, SW, Q), 1.0, 6.0, ((0, 8), (1, 2)))
    query_feats = noise(part_keys[1], (Q, CH), 1.0, 6.0, ((0, 4),))
    support_feats = noise(part_keys[2], (SH, SW, CH), 1.0, 6.0, ((0, 8), (1, 2)))
    query_kernel = noise(arg_keys[3], (3, 3), 9 ** -0.5, 2.0, (), jnp.float32)
    support_kernel = noise(arg_keys[4], (3, 3), 9 ** -0.5, 2.0, (), jnp.float32)
    return {"grad_volume": grad_volume, "query_feats": query_feats, "support_feats": support_feats, "query_kernel": query_kernel, "support_kernel": support_kernel}


def query_pass(volume, kernel):
    planes, columns, queries = volume.shape
    grid = volume.astype(jnp.float32).reshape(planes, columns, QH, QW)
    padded = jnp.pad(grid, ((0, 0), (0, 0), (1, 1), (1, 1)))
    total = jnp.zeros_like(grid)
    for row_shift in range(3):
        for col_shift in range(3):
            total = total + kernel[row_shift, col_shift] * padded[:, :, row_shift:row_shift + QH, col_shift:col_shift + QW]
    return total.reshape(planes, columns, queries)

def support_pass(rimmed, kernel, planes, columns):
    total = jnp.zeros((planes, columns, rimmed.shape[2]), jnp.float32)
    for row_shift in range(3):
        for col_shift in range(3):
            total = total + kernel[row_shift, col_shift] * rimmed[row_shift:row_shift + planes, col_shift:col_shift + columns].astype(jnp.float32)
    return total

def reference(grad_volume, query_feats, support_feats, query_kernel, support_kernel):
    padded = jnp.pad(grad_volume, ((1, 1), (1, 1), (0, 0)))

    def one_row(row_index):
        window = lax.dynamic_slice_in_dim(padded, row_index, 3, 0)
        center = window[1:2, 1:-1]
        summed = query_pass(center, query_kernel) + support_pass(window, support_kernel, 1, SW)
        return summed[0].astype(jnp.bfloat16)
    corr_grad = lax.map(one_row, jnp.arange(SH, dtype=jnp.int32))
    flat = corr_grad.reshape(SH * SW, Q)
    scale_factor = 1.0 / math.sqrt(CH)
    query_grad = lax.dot_general(flat, support_feats.reshape(SH * SW, CH), (((0,), (0,)), ((), ())), preferred_element_type=jnp.float32) * scale_factor
    support_grad = jnp.dot(flat, query_feats, preferred_element_type=jnp.float32) * scale_factor
    return (query_grad, support_grad.reshape(SH, SW, CH))
```

```python
import math

import jax
import jax.numpy as jnp
from jax import lax
from jax.experimental import pallas as pl
from jax.experimental.pallas import tpu as pltpu
from jax.sharding import PartitionSpec as P

QW = 128
QH = 64


def extended(cells, sides, width):
    for axis, dim in sides:
        count = lax.axis_size(axis)
        ends = count - 1
        head = lax.slice_in_dim(cells, 0, width, axis=dim)
        tail = lax.slice_in_dim(cells, cells.shape[dim] - width, cells.shape[dim], axis=dim)
        cells = jnp.concatenate(
            [
                lax.ppermute(tail, axis, [(i, (i + 1) % count) for i in range(ends)]),
                cells,
                lax.ppermute(head, axis, [((i + 1) % count, i) for i in range(ends)]),
            ],
            axis=dim,
        )
    return cells


def shifted(value, axis, steps):
    count = lax.axis_size(axis)
    pairs = [(source, (source + steps) % count) for source in range(count)]
    return lax.ppermute(value, axis, pairs)


def query_pass(volume, kernel):
    planes, columns, queries = volume.shape
    grid = volume.astype(jnp.float32).reshape(planes, columns, QH, QW)
    padded = jnp.pad(grid, ((0, 0), (0, 0), (1, 1), (1, 1)))
    total = jnp.zeros_like(grid)
    for row_shift in range(3):
        for col_shift in range(3):
            total = (
                total
                + kernel[row_shift, col_shift]
                * padded[:, :, row_shift : row_shift + QH, col_shift : col_shift + QW]
            )
    return total.reshape(planes, columns, queries)


def support_pass(rimmed, kernel, planes, columns):
    total = jnp.zeros((planes, columns, rimmed.shape[2]), jnp.float32)
    for row_shift in range(3):
        for col_shift in range(3):
            total = total + kernel[row_shift, col_shift] * rimmed[
                row_shift : row_shift + planes, col_shift : col_shift + columns
            ].astype(jnp.float32)
    return total


def ring_shards(grad_volume, query_feats, support_feats, query_kernel, support_kernel):
    planes, columns, queries = grad_volume.shape
    rimmed = extended(grad_volume, ((("blk", "sub"), 0), ("pair", 1)), 1)
    corr_grad = (
        query_pass(grad_volume, query_kernel)
        + support_pass(rimmed, support_kernel, planes, columns)
    ).astype(jnp.bfloat16)
    moved = lax.all_to_all(corr_grad, "blk", split_axis=2, concat_axis=0, tiled=True)
    cycle_size = lax.axis_size("blk")
    own_index = lax.axis_index("blk")
    tile_len = moved.shape[2]
    tiles = moved.reshape(cycle_size, planes, columns, tile_len)
    width = query_feats.shape[1]
    scale_factor = 1.0 / math.sqrt(width)

    def project(piece_index, feat_piece, acc_piece, count):
        whole_block = lax.dynamic_index_in_dim(tiles, piece_index, 0, keepdims=False)
        block = whole_block.reshape(planes * count, tile_len)
        feat_flat = feat_piece.reshape(planes * count, width)
        query_term = lax.dot_general(
            block, feat_flat, (((0,), (0,)), ((), ())), preferred_element_type=jnp.float32
        )
        acc_new = acc_piece + jnp.dot(
            block, query_feats, preferred_element_type=jnp.float32
        ).reshape(planes, count, width)
        return (query_term, acc_new)

    query_start = jnp.zeros((tile_len, width), jnp.float32)

    def turn_one(turn_index, carry):
        query_total, feat_piece, acc_piece = carry
        term_piece, acc_piece = project(
            (own_index - turn_index) % cycle_size, feat_piece, acc_piece, columns
        )
        feat_piece = shifted(feat_piece, "blk", 1)
        acc_piece = shifted(acc_piece, "blk", 1)
        return (query_total + term_piece, feat_piece, acc_piece)

    start = (query_start, support_feats, jnp.zeros((planes, columns, width), jnp.float32))
    query_total, feat_piece, support_total = lax.fori_loop(0, cycle_size, turn_one, start)
    query_grad = (
        lax.psum_scatter(query_total, ("sub", "pair"), scatter_dimension=0, tiled=True)
        * scale_factor
    )
    return (query_grad, support_total * scale_factor)


def split_taps(kernel):
    high = lax.reduce_precision(kernel, 8, 7)
    return high, kernel - high


def tap_matrix(taps, row_step, col_step):
    total = jnp.zeros(row_step.shape, jnp.float32)
    for a in range(3):
        for b in range(3):
            hit = (row_step == a - 1) & (col_step == b - 1)
            total = jnp.where(hit, taps[a, b], total)
    return total.astype(jnp.bfloat16)


def query_matrices(kernel):
    shape = (4 * QW, 2 * QW)
    source = lax.broadcasted_iota(jnp.int32, shape, 0)
    target = lax.broadcasted_iota(jnp.int32, shape, 1)
    row_step = source // QW - target // QW - 1
    col_step = source % QW - target % QW
    return [tap_matrix(taps, row_step, col_step) for taps in split_taps(kernel)]


def support_matrices(kernel, own, core, count, columns, edge):
    cells = count * columns
    shape = (cells, cells + edge)
    target = lax.broadcasted_iota(jnp.int32, shape, 0)
    source = lax.broadcasted_iota(jnp.int32, shape, 1)
    rim = source >= cells
    slot = jnp.where(rim, source - cells, source // columns)
    beside = jnp.where(core == 0, columns, -1)
    column = jnp.where(rim, beside, source % columns)
    row_step = (own ^ slot) - (own ^ (target // columns))
    row_step = jnp.where(slot < count, row_step, 2)
    col_step = column - target % columns
    return [tap_matrix(taps, row_step, col_step) for taps in split_taps(kernel)]


def tile_kernel(count, columns, tile, edge, width, *refs):
    side_ref = refs[0]
    pieces = refs[1 : 1 + count]
    rim_ref, th_ref, tl_ref, wh_ref, wl_ref, feats_ref = refs[1 + count : 7 + count]
    keep_ref, send_ref, own_ref = refs[7 + count : 10 + count]
    parts = refs[10 + count : 9 + 2 * count]
    cells_ref, corr_ref, feats, sem = refs[9 + 2 * count :]
    cells = count * columns
    side = side_ref[0]
    core = side_ref[1]
    start = pl.multiple_of(side * tile, tile)
    fetch = pltpu.make_async_copy(feats_ref.at[pl.ds(start, tile), :], feats, sem)
    fetch.start()
    for k in range(count):
        cells_ref[k * columns : (k + 1) * columns, :] = pieces[k][...]
    cells_ref[cells:, QW : QW + tile] = rim_ref[...]
    step = 2 * QW
    for low in range(0, tile, step):
        window = cells_ref[:cells, low : low + 2 * step]
        middle = cells_ref[:, low + QW : low + QW + step]
        total = jnp.dot(window, wh_ref[...], preferred_element_type=jnp.float32)
        total += jnp.dot(window, wl_ref[...], preferred_element_type=jnp.float32)
        total += jnp.dot(th_ref[...], middle, preferred_element_type=jnp.float32)
        total += jnp.dot(tl_ref[...], middle, preferred_element_type=jnp.float32)
        corr_ref[:, low : low + step] = total.astype(jnp.bfloat16)
    half = tile // 2
    keep_ref[...] = corr_ref[:, pl.ds(pl.multiple_of(core * half, half), half)]
    send_ref[...] = corr_ref[:, pl.ds(pl.multiple_of((1 - core) * half, half), half)]
    fetch.wait()
    for low in range(0, width, step):
        total = jnp.dot(
            corr_ref[...], feats[:, low : low + step], preferred_element_type=jnp.float32
        )
        own_ref[:, low : low + step] = total[:columns]
        for k in range(1, count):
            parts[k - 1][:, low : low + step] = total[k * columns : (k + 1) * columns].astype(
                jnp.bfloat16
            )


def tile_call(side, pieces, rim, support_mats, query_mats, feats, count, columns, tile):
    width = feats.shape[1]
    edge = rim.shape[0]
    cells = count * columns
    vmem = pl.BlockSpec(memory_space=pltpu.VMEM)
    flops = 2 * cells * tile * (2 * (cells + edge) + 8 * QW + width)
    moved = 2 * (2 * cells * tile + 4 * cells * cells + tile * width + cells * width)
    return pl.pallas_call(
        lambda *refs: tile_kernel(count, columns, tile, edge, width, *refs),
        out_shape=[
            jax.ShapeDtypeStruct((cells, tile // 2), jnp.bfloat16),
            jax.ShapeDtypeStruct((cells, tile // 2), jnp.bfloat16),
            jax.ShapeDtypeStruct((columns, width), jnp.float32),
        ]
        + [jax.ShapeDtypeStruct((columns, width), jnp.bfloat16)] * (count - 1),
        in_specs=[pl.BlockSpec(memory_space=pltpu.SMEM)]
        + [vmem] * (count + 5)
        + [pl.BlockSpec(memory_space=pl.ANY)],
        out_specs=[vmem] * (count + 2),
        scratch_shapes=[
            pltpu.VMEM((cells + edge, tile + 2 * QW), jnp.bfloat16),
            pltpu.VMEM((cells, tile), jnp.bfloat16),
            pltpu.VMEM((tile, width), jnp.bfloat16),
            pltpu.SemaphoreType.DMA,
        ],
        compiler_params=pltpu.CompilerParams(vmem_limit_bytes=40 << 20),
        cost_estimate=pl.CostEstimate(flops=flops, bytes_accessed=moved, transcendentals=0),
        name="tile_kernel",
    )(side, *pieces, rim, *support_mats, *query_mats, feats)


def gathered(feats, count, columns, bits):
    held = {0: feats}
    for bit in bits:
        slots = sorted(held)
        block = jnp.concatenate([held[k] for k in slots], axis=0) if len(slots) > 1 else held[0]
        moved = lax.ppermute(block, ("blk", "sub"), [(i, i ^ bit) for i in range(count)])
        for at, k in enumerate(slots):
            held[k ^ bit] = moved[at * columns : (at + 1) * columns]
    return jnp.concatenate([held[k] for k in range(count)], axis=0)


def tile_shards(grad_volume, query_feats, support_feats, query_kernel, support_kernel):
    _, columns, queries = grad_volume.shape
    width = query_feats.shape[1]
    outer = lax.axis_size("blk")
    inner = lax.axis_size("sub")
    count = outer * inner
    tile = queries // count
    scale_factor = 1.0 / math.sqrt(width)
    own = lax.axis_index(("blk", "sub"))
    side = lax.axis_index("sub")
    core = lax.axis_index("pair")
    swap = [(0, 1), (1, 0)]

    def exchanged(value, mask):
        return lax.ppermute(value, ("blk", "sub"), [(i, i ^ mask) for i in range(count)])

    volume = jnp.pad(grad_volume[0], ((0, 0), (QW, QW)))

    def piece(mask):
        return lax.dynamic_slice(volume, (0, (own ^ mask) * tile), (columns, tile + 2 * QW))

    pieces = [piece(0)] + [None] * (count - 1)
    for mask in range(count - 1, 0, -1):
        pieces[mask] = exchanged(piece(mask), mask)

    bits = []
    bit = count // 2
    while bit:
        bits.append(bit)
        bit //= 2
    feats_own = gathered(support_feats[0], count, columns, bits)
    feats_other = lax.ppermute(feats_own, "pair", swap)

    edge = 16 * -(-count // 16)
    border = jnp.where(core == 0, columns - 1, 0)
    rim = jnp.concatenate(
        [lax.dynamic_slice(cell, (border, QW), (1, tile)) for cell in pieces]
        + [jnp.zeros((edge - count, tile), jnp.bfloat16)],
        axis=0,
    )
    rim = lax.ppermute(rim, "pair", swap)
    outs = tile_call(
        jnp.stack([side, core]).astype(jnp.int32),
        pieces,
        rim,
        support_matrices(support_kernel, own, core, count, columns, edge),
        query_matrices(query_kernel),
        query_feats,
        count,
        columns,
        tile,
    )
    keep, send, support_own = outs[:3]
    parts = outs[3:]
    landed = [exchanged(parts[mask - 1], mask) for mask in range(count - 1, 0, -1)]
    other = lax.ppermute(send, "pair", swap)

    def query_term(block, feats):
        return lax.dot_general(
            block, feats, (((0,), (0,)), ((), ())), preferred_element_type=jnp.float32
        )

    query_grad = (query_term(keep, feats_own) + query_term(other, feats_other)) * scale_factor
    support_grad = support_own
    for term in landed:
        support_grad = support_grad + term.astype(jnp.float32)
    return (query_grad, (support_grad * scale_factor)[None])


def tiles_fit(mesh, grad_volume):
    shape = dict(mesh.shape)
    count = shape["blk"] * shape["sub"]
    planes = grad_volume.shape[0] // (shape["grp"] * count)
    columns = grad_volume.shape[1] // shape["pair"]
    return (
        planes == 1
        and shape["pair"] == 2
        and count & (count - 1) == 0
        and count * columns <= 1024
        and columns % 16 == 0
        and QH * QW % (count * 2 * QW) == 0
    )


def solution(mesh):
    in_specs = (
        P(("grp", "blk", "sub"), "pair", None),
        P(("grp", "blk"), None),
        P(("grp", "blk", "sub"), "pair", None),
        P(),
        P(),
    )
    out_specs = (P(("grp", "blk", "sub", "pair"), None), P(("grp", "blk", "sub"), "pair", None))

    def program(grad_volume, *rest):
        body = tile_shards if tiles_fit(mesh, grad_volume) else ring_shards
        mapped = jax.shard_map(
            body, mesh=mesh, in_specs=in_specs, out_specs=out_specs, check_vma=False
        )
        return mapped(grad_volume, *rest)

    return program
```

```python
import math

import jax
import jax.numpy as jnp
from jax import lax
from jax.experimental import pallas as pl
from jax.experimental.pallas import tpu as pltpu
from jax.sharding import PartitionSpec as P

QW = 128
QH = 64


def extended(cells, sides, width):
    for axis, dim in sides:
        count = lax.axis_size(axis)
        ends = count - 1
        head = lax.slice_in_dim(cells, 0, width, axis=dim)
        tail = lax.slice_in_dim(cells, cells.shape[dim] - width, cells.shape[dim], axis=dim)
        cells = jnp.concatenate(
            [
                lax.ppermute(tail, axis, [(i, (i + 1) % count) for i in range(ends)]),
                cells,
                lax.ppermute(head, axis, [((i + 1) % count, i) for i in range(ends)]),
            ],
            axis=dim,
        )
    return cells


def shifted(value, axis, steps):
    count = lax.axis_size(axis)
    pairs = [(source, (source + steps) % count) for source in range(count)]
    return lax.ppermute(value, axis, pairs)


def query_pass(volume, kernel):
    planes, columns, queries = volume.shape
    grid = volume.astype(jnp.float32).reshape(planes, columns, QH, QW)
    padded = jnp.pad(grid, ((0, 0), (0, 0), (1, 1), (1, 1)))
    total = jnp.zeros_like(grid)
    for row_shift in range(3):
        for col_shift in range(3):
            total = (
                total
                + kernel[row_shift, col_shift]
                * padded[:, :, row_shift : row_shift + QH, col_shift : col_shift + QW]
            )
    return total.reshape(planes, columns, queries)


def support_pass(rimmed, kernel, planes, columns):
    total = jnp.zeros((planes, columns, rimmed.shape[2]), jnp.float32)
    for row_shift in range(3):
        for col_shift in range(3):
            total = total + kernel[row_shift, col_shift] * rimmed[
                row_shift : row_shift + planes, col_shift : col_shift + columns
            ].astype(jnp.float32)
    return total


def ring_shards(grad_volume, query_feats, support_feats, query_kernel, support_kernel):
    planes, columns, queries = grad_volume.shape
    rimmed = extended(grad_volume, ((("blk", "sub"), 0), ("pair", 1)), 1)
    corr_grad = (
        query_pass(grad_volume, query_kernel)
        + support_pass(rimmed, support_kernel, planes, columns)
    ).astype(jnp.bfloat16)
    moved = lax.all_to_all(corr_grad, "blk", split_axis=2, concat_axis=0, tiled=True)
    cycle_size = lax.axis_size("blk")
    own_index = lax.axis_index("blk")
    tile_len = moved.shape[2]
    tiles = moved.reshape(cycle_size, planes, columns, tile_len)
    width = query_feats.shape[1]
    scale_factor = 1.0 / math.sqrt(width)

    def project(piece_index, feat_piece, acc_piece, count):
        whole_block = lax.dynamic_index_in_dim(tiles, piece_index, 0, keepdims=False)
        block = whole_block.reshape(planes * count, tile_len)
        feat_flat = feat_piece.reshape(planes * count, width)
        query_term = lax.dot_general(
            block, feat_flat, (((0,), (0,)), ((), ())), preferred_element_type=jnp.float32
        )
        acc_new = acc_piece + jnp.dot(
            block, query_feats, preferred_element_type=jnp.float32
        ).reshape(planes, count, width)
        return (query_term, acc_new)

    query_start = jnp.zeros((tile_len, width), jnp.float32)

    def turn_one(turn_index, carry):
        query_total, feat_piece, acc_piece = carry
        term_piece, acc_piece = project(
            (own_index - turn_index) % cycle_size, feat_piece, acc_piece, columns
        )
        feat_piece = shifted(feat_piece, "blk", 1)
        acc_piece = shifted(acc_piece, "blk", 1)
        return (query_total + term_piece, feat_piece, acc_piece)

    start = (query_start, support_feats, jnp.zeros((planes, columns, width), jnp.float32))
    query_total, feat_piece, support_total = lax.fori_loop(0, cycle_size, turn_one, start)
    query_grad = (
        lax.psum_scatter(query_total, ("sub", "pair"), scatter_dimension=0, tiled=True)
        * scale_factor
    )
    return (query_grad, support_total * scale_factor)


def split_taps(kernel):
    high = lax.reduce_precision(kernel, 8, 7)
    return high, kernel - high


def banded(taps, step):
    total = jnp.where(step == 1, taps[2], 0.0)
    return jnp.where(step == 0, taps[1], jnp.where(step == -1, taps[0], total))


def matrix_kernel(count, columns, place_ref, taps_ref, th_ref, tl_ref, wh_ref, wl_ref):
    own = place_ref[0]
    beside = jnp.where(place_ref[1] == 0, columns, -1)
    cells = count * columns

    def taps(part, kernel, a, b):
        return taps_ref[((part * 2 + kernel) * 3 + a) * 3 + b]

    def span(shape, dim):
        return lax.broadcasted_iota(jnp.int32, shape, dim)

    square = (QW, QW)
    step = span(square, 0) - span(square, 1)
    for part, w_ref in enumerate((wh_ref, wl_ref)):
        bands = [
            banded([taps(part, 0, a, b) for b in range(3)], step).astype(jnp.bfloat16)
            for a in range(3)
        ]
        for source in range(4):
            for target in range(2):
                a = source - target
                block = bands[a] if 0 <= a <= 2 else jnp.zeros(square, jnp.bfloat16)
                w_ref[source * QW : (source + 1) * QW, target * QW : (target + 1) * QW] = block
    edge = th_ref.shape[1] - cells
    blocks = [(low, QW) for low in range(0, cells, QW)] + [(cells, edge)]
    for low, lanes in blocks:
        shape = (columns, lanes)
        lane = span(shape, 1)
        if low < cells:
            slot = (lane + low) // columns
            column = lax.rem(lane, columns)
        else:
            slot = lane
            column = jnp.full(shape, beside, jnp.int32)
        step = column - span(shape, 0)
        plane = jnp.where(slot < count, own ^ slot, 2 * count)
        for target in range(count):
            rise = plane - (own ^ target)
            for part, t_ref in enumerate((th_ref, tl_ref)):
                row = [
                    banded([taps(part, 1, a, b) for a in range(3)], rise) for b in range(3)
                ]
                t_ref[target * columns : (target + 1) * columns, low : low + lanes] = banded(
                    row, step
                ).astype(jnp.bfloat16)


def matrix_call(place, query_kernel, support_kernel, count, columns, edge):
    query_parts = split_taps(query_kernel)
    support_parts = split_taps(support_kernel)
    taps = jnp.stack(
        [query_parts[0], support_parts[0], query_parts[1], support_parts[1]]
    ).reshape(-1)
    cells = count * columns
    wide = jax.ShapeDtypeStruct((cells, cells + edge), jnp.bfloat16)
    band = jax.ShapeDtypeStruct((4 * QW, 2 * QW), jnp.bfloat16)
    return pl.pallas_call(
        lambda *refs: matrix_kernel(count, columns, *refs),
        out_shape=[wide, wide, band, band],
        in_specs=[pl.BlockSpec(memory_space=pltpu.SMEM)] * 2,
        out_specs=[pl.BlockSpec(memory_space=pltpu.VMEM)] * 4,
        cost_estimate=pl.CostEstimate(
            flops=20 * cells * cells, bytes_accessed=8 * cells * cells, transcendentals=0
        ),
        compiler_params=pltpu.CompilerParams(vmem_limit_bytes=4 << 20),
        name="matrix_kernel",
    )(place, taps)


def rim_kernel(count, columns, tile, place_ref, *refs):
    pieces, rim_ref = refs[:count], refs[count]
    first = place_ref[1] != 0
    inner = slice(QW, QW + tile)
    rows = []
    for piece in pieces:
        head = piece[:16, inner].astype(jnp.float32)[:1]
        tail = piece[columns - 16 :, inner].astype(jnp.float32)[15:]
        rows.append(jnp.where(first, head, tail))
    empty = rim_ref.shape[0] - count
    if empty:
        rows.append(jnp.zeros((empty, tile), jnp.float32))
    rim_ref[...] = jnp.concatenate(rows, axis=0).astype(jnp.bfloat16)


def rim_call(place, pieces, columns, tile, edge):
    count = len(pieces)
    return pl.pallas_call(
        lambda *refs: rim_kernel(count, columns, tile, *refs),
        out_shape=jax.ShapeDtypeStruct((edge, tile), jnp.bfloat16),
        in_specs=[pl.BlockSpec(memory_space=pltpu.SMEM)]
        + [pl.BlockSpec(memory_space=pltpu.VMEM)] * count,
        out_specs=pl.BlockSpec(memory_space=pltpu.VMEM),
        cost_estimate=pl.CostEstimate(
            flops=count * tile, bytes_accessed=64 * count * tile, transcendentals=0
        ),
        compiler_params=pltpu.CompilerParams(vmem_limit_bytes=4 << 20),
        name="rim_kernel",
    )(place, *pieces)


def tile_kernel(order, columns, tile, edge, width, *refs):
    count = len(order)
    side_ref = refs[0]
    pieces = refs[1 : 1 + count]
    rim_ref, th_ref, tl_ref, wh_ref, wl_ref, feats_ref = refs[1 + count : 7 + count]
    keep_ref, send_ref, own_ref = refs[7 + count : 10 + count]
    parts = refs[10 + count : 9 + 2 * count]
    cells_ref, corr_ref, feats, sem = refs[9 + 2 * count :]
    cells = count * columns
    side = side_ref[0]
    core = side_ref[1]
    start = pl.multiple_of(side * tile, tile)
    fetch = pltpu.make_async_copy(feats_ref.at[pl.ds(start, tile), :], feats, sem)
    fetch.start()
    for k in range(count):
        cells_ref[k * columns : (k + 1) * columns, :] = pieces[k][...]
    cells_ref[cells:, QW : QW + tile] = rim_ref[...]
    step = 2 * QW
    for low in range(0, tile, step):
        window = cells_ref[:cells, low : low + 2 * step]
        middle = cells_ref[:, low + QW : low + QW + step]
        total = jnp.dot(window, wh_ref[...], preferred_element_type=jnp.float32)
        total += jnp.dot(window, wl_ref[...], preferred_element_type=jnp.float32)
        total += jnp.dot(th_ref[...], middle, preferred_element_type=jnp.float32)
        total += jnp.dot(tl_ref[...], middle, preferred_element_type=jnp.float32)
        corr_ref[:, low : low + step] = total.astype(jnp.bfloat16)
    half = tile // 2
    for at, k in enumerate(order):
        source, target = pl.ds(k * columns, columns), pl.ds(at * columns, columns)
        for half_ref, which in ((keep_ref, core), (send_ref, 1 - core)):
            start = pl.multiple_of(which * half, half)
            half_ref[target, :] = corr_ref[source, pl.ds(start, half)]
    fetch.wait()
    for low in range(0, width, step):
        total = jnp.dot(
            corr_ref[...], feats[:, low : low + step], preferred_element_type=jnp.float32
        )
        own_ref[:, low : low + step] = total[:columns]
        for k in range(1, count):
            parts[k - 1][:, low : low + step] = total[k * columns : (k + 1) * columns].astype(
                jnp.bfloat16
            )


def tile_call(side, pieces, rim, support_mats, query_mats, feats, order, columns, tile):
    width = feats.shape[1]
    count = len(order)
    edge = rim.shape[0]
    cells = count * columns
    vmem = pl.BlockSpec(memory_space=pltpu.VMEM)
    flops = 2 * cells * tile * (2 * (cells + edge) + 8 * QW + width)
    moved = 2 * (2 * cells * tile + 4 * cells * cells + tile * width + cells * width)
    return pl.pallas_call(
        lambda *refs: tile_kernel(order, columns, tile, edge, width, *refs),
        out_shape=[
            jax.ShapeDtypeStruct((cells, tile // 2), jnp.bfloat16),
            jax.ShapeDtypeStruct((cells, tile // 2), jnp.bfloat16),
            jax.ShapeDtypeStruct((columns, width), jnp.float32),
        ]
        + [jax.ShapeDtypeStruct((columns, width), jnp.bfloat16)] * (count - 1),
        in_specs=[pl.BlockSpec(memory_space=pltpu.SMEM)]
        + [vmem] * (count + 5)
        + [pl.BlockSpec(memory_space=pltpu.HBM)],
        out_specs=[vmem] * (count + 2),
        scratch_shapes=[
            pltpu.VMEM((cells + edge, tile + 2 * QW), jnp.bfloat16),
            pltpu.VMEM((cells, tile), jnp.bfloat16),
            pltpu.VMEM((tile, width), jnp.bfloat16),
            pltpu.SemaphoreType.DMA,
        ],
        compiler_params=pltpu.CompilerParams(vmem_limit_bytes=20 << 20),
        cost_estimate=pl.CostEstimate(flops=flops, bytes_accessed=moved, transcendentals=0),
        name="tile_kernel",
    )(side, *pieces, rim, *support_mats, *query_mats, feats)


def tile_shards(grad_volume, query_feats, support_feats, query_kernel, support_kernel):
    _, columns, queries = grad_volume.shape
    width = query_feats.shape[1]
    outer = lax.axis_size("blk")
    inner = lax.axis_size("sub")
    count = outer * inner
    tile = queries // count
    cells = count * columns
    scale_factor = 1.0 / math.sqrt(width)
    own = lax.axis_index(("blk", "sub"))
    side = lax.axis_index("sub")
    core = lax.axis_index("pair")
    swap = [(0, 1), (1, 0)]

    def exchanged(value, mask):
        return lax.ppermute(value, ("blk", "sub"), [(i, i ^ mask) for i in range(count)])

    volume = jnp.pad(grad_volume[0], ((0, 0), (QW, QW)))

    def piece(mask):
        return lax.dynamic_slice(volume, (0, (own ^ mask) * tile), (columns, tile + 2 * QW))

    pieces = [piece(0)] + [None] * (count - 1)
    for mask in range(count - 1, 0, -1):
        pieces[mask] = exchanged(piece(mask), mask)

    feats_near = support_feats[0]
    order = [0]
    bit = count // 2
    while bit > 1:
        feats_near = jnp.concatenate([feats_near, exchanged(feats_near, bit)])
        order += [k ^ bit for k in order]
        bit //= 2
    order += [k ^ 1 for k in order]
    feats_far = exchanged(feats_near, 1)
    near_other = lax.ppermute(feats_near, "pair", swap)

    edge = 16 * -(-count // 16)
    place = jnp.stack([own, core]).astype(jnp.int32)
    rim = lax.ppermute(rim_call(place, pieces, columns, tile, edge), "pair", swap)
    mats = matrix_call(place, query_kernel, support_kernel, count, columns, edge)
    outs = tile_call(
        jnp.stack([side, core]).astype(jnp.int32),
        pieces,
        rim,
        mats[:2],
        mats[2:],
        query_feats,
        order,
        columns,
        tile,
    )
    keep, send, support_own = outs[:3]
    feats_far, keep = lax.optimization_barrier((feats_far, keep))
    far_other = lax.ppermute(feats_far, "pair", swap)
    parts = outs[3:]
    landed = [exchanged(parts[mask - 1], mask) for mask in range(count - 1, 0, -1)]
    other = lax.ppermute(send, "pair", swap)

    def query_term(block, feats):
        return lax.dot_general(
            block, feats, (((0,), (0,)), ((), ())), preferred_element_type=jnp.float32
        )

    near = cells // 2
    query_grad = query_term(keep[:near], feats_near)
    query_grad += query_term(other[:near], near_other)
    query_grad += query_term(keep[near:], feats_far)
    query_grad += query_term(other[near:], far_other)
    query_grad *= scale_factor
    landed, query_grad = lax.optimization_barrier((landed, query_grad))
    support_grad = support_own
    for term in landed:
        support_grad = support_grad + term.astype(jnp.float32)
    return (query_grad, (support_grad * scale_factor)[None])


def tiles_fit(mesh, grad_volume):
    shape = dict(mesh.shape)
    count = shape["blk"] * shape["sub"]
    planes = grad_volume.shape[0] // (shape["grp"] * count)
    columns = grad_volume.shape[1] // shape["pair"]
    return (
        planes == 1
        and shape["pair"] == 2
        and count & (count - 1) == 0
        and count * columns <= 1024
        and columns % 16 == 0
        and QW % columns == 0
        and count * columns % QW == 0
        and QH * QW % (count * 2 * QW) == 0
    )


def solution(mesh):
    in_specs = (
        P(("grp", "blk", "sub"), "pair", None),
        P(("grp", "blk"), None),
        P(("grp", "blk", "sub"), "pair", None),
        P(),
        P(),
    )
    out_specs = (P(("grp", "blk", "sub", "pair"), None), P(("grp", "blk", "sub"), "pair", None))

    def program(grad_volume, *rest):
        body = tile_shards if tiles_fit(mesh, grad_volume) else ring_shards
        mapped = jax.shard_map(
            body, mesh=mesh, in_specs=in_specs, out_specs=out_specs, check_vma=False
        )
        return mapped(grad_volume, *rest)

    return program
```

```python
import math

import jax
import jax.numpy as jnp
from jax import lax
from jax.experimental import pallas as pl
from jax.experimental.pallas import tpu as pltpu
from jax.sharding import PartitionSpec as P

QW = 128
QH = 64


def extended(cells, sides, width):
    for axis, dim in sides:
        count = lax.axis_size(axis)
        ends = count - 1
        head = lax.slice_in_dim(cells, 0, width, axis=dim)
        tail = lax.slice_in_dim(cells, cells.shape[dim] - width, cells.shape[dim], axis=dim)
        cells = jnp.concatenate(
            [
                lax.ppermute(tail, axis, [(i, (i + 1) % count) for i in range(ends)]),
                cells,
                lax.ppermute(head, axis, [((i + 1) % count, i) for i in range(ends)]),
            ],
            axis=dim,
        )
    return cells


def shifted(value, axis, steps):
    count = lax.axis_size(axis)
    pairs = [(source, (source + steps) % count) for source in range(count)]
    return lax.ppermute(value, axis, pairs)


def query_pass(volume, kernel):
    planes, columns, queries = volume.shape
    grid = volume.astype(jnp.float32).reshape(planes, columns, QH, QW)
    padded = jnp.pad(grid, ((0, 0), (0, 0), (1, 1), (1, 1)))
    total = jnp.zeros_like(grid)
    for row_shift in range(3):
        for col_shift in range(3):
            total = (
                total
                + kernel[row_shift, col_shift]
                * padded[:, :, row_shift : row_shift + QH, col_shift : col_shift + QW]
            )
    return total.reshape(planes, columns, queries)


def support_pass(rimmed, kernel, planes, columns):
    total = jnp.zeros((planes, columns, rimmed.shape[2]), jnp.float32)
    for row_shift in range(3):
        for col_shift in range(3):
            total = total + kernel[row_shift, col_shift] * rimmed[
                row_shift : row_shift + planes, col_shift : col_shift + columns
            ].astype(jnp.float32)
    return total


def ring_shards(grad_volume, query_feats, support_feats, query_kernel, support_kernel):
    planes, columns, queries = grad_volume.shape
    rimmed = extended(grad_volume, ((("blk", "sub"), 0), ("pair", 1)), 1)
    corr_grad = (
        query_pass(grad_volume, query_kernel)
        + support_pass(rimmed, support_kernel, planes, columns)
    ).astype(jnp.bfloat16)
    moved = lax.all_to_all(corr_grad, "blk", split_axis=2, concat_axis=0, tiled=True)
    cycle_size = lax.axis_size("blk")
    own_index = lax.axis_index("blk")
    tile_len = moved.shape[2]
    tiles = moved.reshape(cycle_size, planes, columns, tile_len)
    width = query_feats.shape[1]
    scale_factor = 1.0 / math.sqrt(width)

    def project(piece_index, feat_piece, acc_piece, count):
        whole_block = lax.dynamic_index_in_dim(tiles, piece_index, 0, keepdims=False)
        block = whole_block.reshape(planes * count, tile_len)
        feat_flat = feat_piece.reshape(planes * count, width)
        query_term = lax.dot_general(
            block, feat_flat, (((0,), (0,)), ((), ())), preferred_element_type=jnp.float32
        )
        acc_new = acc_piece + jnp.dot(
            block, query_feats, preferred_element_type=jnp.float32
        ).reshape(planes, count, width)
        return (query_term, acc_new)

    query_start = jnp.zeros((tile_len, width), jnp.float32)

    def turn_one(turn_index, carry):
        query_total, feat_piece, acc_piece = carry
        term_piece, acc_piece = project(
            (own_index - turn_index) % cycle_size, feat_piece, acc_piece, columns
        )
        feat_piece = shifted(feat_piece, "blk", 1)
        acc_piece = shifted(acc_piece, "blk", 1)
        return (query_total + term_piece, feat_piece, acc_piece)

    start = (query_start, support_feats, jnp.zeros((planes, columns, width), jnp.float32))
    query_total, feat_piece, support_total = lax.fori_loop(0, cycle_size, turn_one, start)
    query_grad = (
        lax.psum_scatter(query_total, ("sub", "pair"), scatter_dimension=0, tiled=True)
        * scale_factor
    )
    return (query_grad, support_total * scale_factor)


def split_taps(kernel):
    high = lax.reduce_precision(kernel, 8, 7)
    return high, kernel - high


def banded(taps, step):
    total = jnp.where(step == 1, taps[2], 0.0)
    return jnp.where(step == 0, taps[1], jnp.where(step == -1, taps[0], total))


def matrix_kernel(count, columns, place_ref, taps_ref, t_ref, rim_ref, wh_ref, wl_ref):
    cells = count * columns

    def taps(part, kernel, a, b):
        return taps_ref[((part * 2 + kernel) * 3 + a) * 3 + b]

    def span(shape, dim):
        return lax.broadcasted_iota(jnp.int32, shape, dim)

    square = (QW, QW)
    step = span(square, 0) - span(square, 1)
    for part, w_ref in enumerate((wh_ref, wl_ref)):
        bands = [
            banded([taps(part, 0, a, b) for b in range(3)], step).astype(jnp.bfloat16)
            for a in range(3)
        ]
        for source in range(4):
            for target in range(2):
                a = source - target
                block = bands[a] if 0 <= a <= 2 else jnp.zeros(square, jnp.bfloat16)
                w_ref[source * QW : (source + 1) * QW, target * QW : (target + 1) * QW] = block
    group = 4 * columns
    shape = (2 * columns, group)
    row_step = span(shape, 1) // columns - span(shape, 0) // columns - 1
    col_step = lax.rem(span(shape, 1), columns) - lax.rem(span(shape, 0), columns)
    beside = jnp.where(place_ref[1] == 0, columns, -1)
    rim_shape = (cells, rim_ref.shape[1] // 2)
    rim_row = span(rim_shape, 1) - span(rim_shape, 0) // columns
    rim_col = beside - lax.rem(span(rim_shape, 0), columns)
    for part in range(2):
        rows = [
            banded([taps(part, 1, a, b) for a in range(3)], row_step) for b in range(3)
        ]
        block = banded(rows, col_step).astype(jnp.bfloat16)
        t_ref[part * 2 * columns : (part + 1) * 2 * columns, :] = block
        rows = [banded([taps(part, 1, a, b) for a in range(3)], rim_row) for b in range(3)]
        block = banded(rows, rim_col).astype(jnp.bfloat16)
        rim_ref[:, part * rim_shape[1] : (part + 1) * rim_shape[1]] = block


def matrix_call(place, query_kernel, support_kernel, count, columns, edge):
    query_parts = split_taps(query_kernel)
    support_parts = split_taps(support_kernel)
    taps = jnp.stack(
        [query_parts[0], support_parts[0], query_parts[1], support_parts[1]]
    ).reshape(-1)
    shapes = [
        (4 * columns, 4 * columns),
        (count * columns, 2 * edge),
        (4 * QW, 2 * QW),
        (4 * QW, 2 * QW),
    ]
    return pl.pallas_call(
        lambda *refs: matrix_kernel(count, columns, *refs),
        out_shape=[jax.ShapeDtypeStruct(shape, jnp.bfloat16) for shape in shapes],
        in_specs=[pl.BlockSpec(memory_space=pltpu.SMEM)] * 2,
        out_specs=[pl.BlockSpec(memory_space=pltpu.VMEM)] * 4,
        cost_estimate=pl.CostEstimate(
            flops=20 * QW * QW * count, bytes_accessed=32 * QW * QW, transcendentals=0
        ),
        compiler_params=pltpu.CompilerParams(vmem_limit_bytes=4 << 20),
        name="matrix_kernel",
    )(place, taps)


def gather_kernel(count, columns, tile, place_ref, *refs):
    pieces, cells_ref, rim_ref = refs[:count], refs[count], refs[count + 1]
    own = place_ref[0]
    first = place_ref[1] != 0
    inner = slice(QW, QW + tile)
    empty = jnp.zeros((columns, tile + 2 * QW), jnp.bfloat16)
    cells_ref[:columns, :] = empty
    cells_ref[(count + 1) * columns :, :] = empty
    edge = rim_ref.shape[0] // 2
    span = lax.broadcasted_iota(jnp.int32, (edge, tile), 0)
    total = jnp.zeros(span.shape, jnp.float32)
    for k, piece in enumerate(reversed(pieces)):
        start = pl.multiple_of(((own ^ k) + 1) * columns, columns)
        cells_ref[pl.ds(start, columns), :] = piece[...]
        head = piece[:16, inner].astype(jnp.float32)[:1]
        tail = piece[columns - 16 :, inner].astype(jnp.float32)[15:]
        row = jnp.where(first, head, tail)
        total = jnp.where(span == (own ^ k), row, total)
    rim_ref[:edge, :] = total.astype(jnp.bfloat16)
    rim_ref[edge:, :] = total.astype(jnp.bfloat16)


def gather_call(place, pieces, tile, edge):
    count = len(pieces)
    columns, reach = pieces[0].shape
    return pl.pallas_call(
        lambda *refs: gather_kernel(count, columns, tile, *refs),
        out_shape=[
            jax.ShapeDtypeStruct(((count + 2) * columns, reach), jnp.bfloat16),
            jax.ShapeDtypeStruct((2 * edge, tile), jnp.bfloat16),
        ],
        in_specs=[pl.BlockSpec(memory_space=pltpu.SMEM)]
        + [pl.BlockSpec(memory_space=pltpu.VMEM)] * count,
        out_specs=[pl.BlockSpec(memory_space=pltpu.VMEM)] * 2,
        compiler_params=pltpu.CompilerParams(vmem_limit_bytes=4 << 20),
        cost_estimate=pl.CostEstimate(
            flops=count * tile, bytes_accessed=4 * count * columns * reach, transcendentals=0
        ),
        name="gather_kernel",
    )(place, *reversed(pieces))


def product(left, right):
    return jnp.dot(left, right, preferred_element_type=jnp.float32)


def corr_kernel(
    group, columns, tile, place_ref, cells_ref, rim_ref, t_ref, edge_ref, wh_ref, wl_ref,
    move_ref, stay_ref, keep_ref, send_ref, corr_ref,
):
    half = corr_ref.shape[0] // columns
    own = place_ref[0]
    core = place_ref[1]
    base = ((own // half) ^ group) * half
    rows = half * columns
    pair = 2 * columns

    def plane_rows(plane, size):
        return pl.ds(pl.multiple_of(plane * columns, columns), size)

    step = 2 * QW
    for low in range(0, tile, step):
        window = cells_ref[plane_rows(base + 1, rows), low : low + 2 * step]
        total = product(window, wh_ref[...]) + product(window, wl_ref[...])
        edges = edge_ref[plane_rows(base, rows), :]
        total += product(edges, rim_ref[:, low : low + step])
        for at in range(0, half, 2):
            middle = cells_ref[plane_rows(base + at, 2 * pair), low + QW : low + QW + step]
            both = product(t_ref[...], middle)
            top = at * columns
            block = total[top : top + pair] + both[:pair] + both[pair:]
            corr_ref[top : top + pair, low : low + step] = block.astype(jnp.bfloat16)
    width = tile // 2
    for k in range(half):
        source = plane_rows(lax.rem(own, half) ^ k, columns)
        out_ref = move_ref if k % 2 else stay_ref
        out_ref[k // 2 * columns : (k // 2 + 1) * columns, :] = corr_ref[source, :]
        for half_ref, which in ((keep_ref, core), (send_ref, 1 - core)):
            start = pl.multiple_of(which * width, width)
            half_ref[k * columns : (k + 1) * columns, :] = corr_ref[source, pl.ds(start, width)]


def corr_call(group, place, cells, rim, mats, count):
    tile = rim.shape[1]
    columns = cells.shape[0] // (count + 2)
    half = count // 2
    rows = half * columns
    vmem = pl.BlockSpec(memory_space=pltpu.VMEM)
    wide = jax.ShapeDtypeStruct((rows // 2, tile), jnp.bfloat16)
    tall = jax.ShapeDtypeStruct((rows, tile // 2), jnp.bfloat16)
    return pl.pallas_call(
        lambda *refs: corr_kernel(group, columns, tile, *refs),
        out_shape=[wide, wide, tall, tall],
        in_specs=[pl.BlockSpec(memory_space=pltpu.SMEM)] + [vmem] * 6,
        out_specs=[vmem] * 4,
        scratch_shapes=[pltpu.VMEM((rows, tile), jnp.bfloat16)],
        compiler_params=pltpu.CompilerParams(vmem_limit_bytes=6 << 20),
        cost_estimate=pl.CostEstimate(
            flops=2 * rows * tile * (8 * columns + 8 * QW),
            bytes_accessed=8 * rows * tile,
            transcendentals=0,
        ),
        name="corr_kernel",
    )(place, cells, rim, *mats)


def partial_kernel(columns, stay_ref, moved_ref, here_ref, there_ref, *outs):
    width = here_ref.shape[1]
    step = 2 * QW
    for low in range(0, width, step):
        lanes = slice(low, low + step)
        total = product(stay_ref[...], here_ref[:, lanes])
        total += product(moved_ref[...], there_ref[:, lanes])
        for k, out_ref in enumerate(outs):
            out_ref[:, lanes] = total[k * columns : (k + 1) * columns].astype(out_ref.dtype)


def partial_call(stay, moved, here, there, columns, types):
    rows, tile = stay.shape
    width = here.shape[1]
    vmem = pl.BlockSpec(memory_space=pltpu.VMEM)
    return pl.pallas_call(
        lambda *refs: partial_kernel(columns, *refs),
        out_shape=[jax.ShapeDtypeStruct((columns, width), kind) for kind in types],
        in_specs=[vmem] * 4,
        out_specs=[vmem] * len(types),
        compiler_params=pltpu.CompilerParams(vmem_limit_bytes=6 << 20),
        cost_estimate=pl.CostEstimate(
            flops=4 * rows * tile * width, bytes_accessed=4 * tile * width, transcendentals=0
        ),
        name="partial_kernel",
    )(stay, moved, here, there)


def stack_call(blocks):
    columns, width = blocks[0].shape

    def kernel(*refs):
        for k in range(len(blocks)):
            refs[-1][k * columns : (k + 1) * columns, :] = refs[k][...]

    vmem = pl.BlockSpec(memory_space=pltpu.VMEM)
    return pl.pallas_call(
        kernel,
        out_shape=jax.ShapeDtypeStruct((len(blocks) * columns, width), jnp.bfloat16),
        in_specs=[vmem] * len(blocks),
        out_specs=vmem,
        compiler_params=pltpu.CompilerParams(vmem_limit_bytes=4 << 20),
        cost_estimate=pl.CostEstimate(
            flops=0, bytes_accessed=4 * len(blocks) * columns * width, transcendentals=0
        ),
        name="stack_kernel",
    )(*blocks)


def tile_shards(grad_volume, query_feats, support_feats, query_kernel, support_kernel):
    _, columns, queries = grad_volume.shape
    width = query_feats.shape[1]
    outer = lax.axis_size("blk")
    inner = lax.axis_size("sub")
    count = outer * inner
    half = count // 2
    tile = queries // count
    scale_factor = 1.0 / math.sqrt(width)
    own = lax.axis_index(("blk", "sub"))
    side = lax.axis_index("sub")
    core = lax.axis_index("pair")
    place = jnp.stack([own, core]).astype(jnp.int32)

    def exchanged(value, mask):
        return lax.ppermute(value, ("blk", "sub"), [(i, i ^ mask) for i in range(count)])

    def swapped(value):
        return lax.ppermute(value, "pair", [(0, 1), (1, 0)])

    volume = jnp.pad(grad_volume[0], ((0, 0), (QW, QW)))

    def piece(mask):
        return lax.dynamic_slice(volume, (0, (own ^ mask) * tile), (columns, tile + 2 * QW))

    pieces = [piece(0)] + [None] * (count - 1)
    for mask in range(count - 1, 0, -1):
        pieces[mask] = exchanged(piece(mask), mask)
    held = [support_feats[0]] + [None] * (count - 1)
    bit = half
    while bit:
        for k in range(0, count, 2 * bit):
            held[k ^ bit] = exchanged(held[k], bit)
        bit //= 2

    edge = 16 * -(-count // 16)
    mats = matrix_call(place, query_kernel, support_kernel, count, columns, edge)
    here = lax.dynamic_slice(query_feats, (side * tile, 0), (tile, width))
    there = lax.dynamic_slice(query_feats, ((side ^ 1) * tile, 0), (tile, width))
    ordered = held + pieces[::-1]
    ordered, mats, here, there = lax.optimization_barrier((ordered, mats, here, there))
    held, pieces = ordered[:count], ordered[count:][::-1]
    cells, rim = gather_call(place, pieces, tile, edge)
    rim = swapped(rim)
    move1, stay1, keep1, send1 = corr_call(1, place, cells, rim, mats, count)
    moved1 = exchanged(move1, 1)
    move0, stay0, keep0, send0 = corr_call(0, place, cells, rim, mats, count)
    moved0 = exchanged(move0, 1)
    other1 = swapped(send1)
    moved1, other1 = lax.optimization_barrier((moved1, other1))
    other0 = swapped(send0)
    feats1, feats0 = stack_call(held[half:]), stack_call(held[:half])
    across1, across0 = swapped(feats1), swapped(feats0)
    moved0, other0, across1 = lax.optimization_barrier((moved0, other0, across1))
    narrow = [jnp.bfloat16] * (count // 4)
    parts1 = partial_call(stay1, moved1, here, there, columns, narrow)
    parts0 = partial_call(stay0, moved0, here, there, columns, [jnp.float32] + narrow[1:])
    landed = [exchanged(part, half + 2 * at) for at, part in enumerate(parts1)]
    landed += [exchanged(part, 2 * at) for at, part in enumerate(parts0) if at]

    def query_term(block, feats):
        return lax.dot_general(
            block, feats, (((0,), (0,)), ((), ())), preferred_element_type=jnp.float32
        )

    query_grad = query_term(keep1, feats1) + query_term(keep0, feats0)
    query_grad += query_term(other1, across1)
    query_grad += query_term(other0, across0)
    query_grad *= scale_factor
    support_grad = parts0[0]
    for term in landed:
        support_grad = support_grad + term.astype(jnp.float32)
    return (query_grad, (support_grad * scale_factor)[None])


def tiles_fit(mesh, grad_volume):
    shape = dict(mesh.shape)
    count = shape["blk"] * shape["sub"]
    planes = grad_volume.shape[0] // (shape["grp"] * count)
    columns = grad_volume.shape[1] // shape["pair"]
    return (
        planes == 1
        and shape["pair"] == 2
        and shape["sub"] == 2
        and count >= 4
        and count & (count - 1) == 0
        and count * columns <= 1024
        and columns % 16 == 0
        and QW % columns == 0
        and count * columns % QW == 0
        and QH * QW % (count * 2 * QW) == 0
    )


def solution(mesh):
    in_specs = (
        P(("grp", "blk", "sub"), "pair", None),
        P(("grp", "blk"), None),
        P(("grp", "blk", "sub"), "pair", None),
        P(),
        P(),
    )
    out_specs = (P(("grp", "blk", "sub", "pair"), None), P(("grp", "blk", "sub"), "pair", None))

    def program(grad_volume, *rest):
        body = tile_shards if tiles_fit(mesh, grad_volume) else ring_shards
        mapped = jax.shard_map(
            body, mesh=mesh, in_specs=in_specs, out_specs=out_specs, check_vma=False
        )
        return mapped(grad_volume, *rest)

    return program
```

```python
import math

import jax
import jax.numpy as jnp
from jax import lax
from jax.experimental import pallas as pl
from jax.experimental.pallas import tpu as pltpu
from jax.sharding import PartitionSpec as P

QW = 128
QH = 64


def extended(cells, sides, width):
    for axis, dim in sides:
        count = lax.axis_size(axis)
        ends = count - 1
        head = lax.slice_in_dim(cells, 0, width, axis=dim)
        tail = lax.slice_in_dim(cells, cells.shape[dim] - width, cells.shape[dim], axis=dim)
        cells = jnp.concatenate(
            [
                lax.ppermute(tail, axis, [(i, (i + 1) % count) for i in range(ends)]),
                cells,
                lax.ppermute(head, axis, [((i + 1) % count, i) for i in range(ends)]),
            ],
            axis=dim,
        )
    return cells


def shifted(value, axis, steps):
    count = lax.axis_size(axis)
    pairs = [(source, (source + steps) % count) for source in range(count)]
    return lax.ppermute(value, axis, pairs)


def query_pass(volume, kernel):
    planes, columns, queries = volume.shape
    grid = volume.astype(jnp.float32).reshape(planes, columns, QH, QW)
    padded = jnp.pad(grid, ((0, 0), (0, 0), (1, 1), (1, 1)))
    total = jnp.zeros_like(grid)
    for row_shift in range(3):
        for col_shift in range(3):
            total = (
                total
                + kernel[row_shift, col_shift]
                * padded[:, :, row_shift : row_shift + QH, col_shift : col_shift + QW]
            )
    return total.reshape(planes, columns, queries)


def support_pass(rimmed, kernel, planes, columns):
    total = jnp.zeros((planes, columns, rimmed.shape[2]), jnp.float32)
    for row_shift in range(3):
        for col_shift in range(3):
            total = total + kernel[row_shift, col_shift] * rimmed[
                row_shift : row_shift + planes, col_shift : col_shift + columns
            ].astype(jnp.float32)
    return total


def ring_shards(grad_volume, query_feats, support_feats, query_kernel, support_kernel):
    planes, columns, queries = grad_volume.shape
    rimmed = extended(grad_volume, ((("blk", "sub"), 0), ("pair", 1)), 1)
    corr_grad = (
        query_pass(grad_volume, query_kernel)
        + support_pass(rimmed, support_kernel, planes, columns)
    ).astype(jnp.bfloat16)
    moved = lax.all_to_all(corr_grad, "blk", split_axis=2, concat_axis=0, tiled=True)
    cycle_size = lax.axis_size("blk")
    own_index = lax.axis_index("blk")
    tile_len = moved.shape[2]
    tiles = moved.reshape(cycle_size, planes, columns, tile_len)
    width = query_feats.shape[1]
    scale_factor = 1.0 / math.sqrt(width)

    def project(piece_index, feat_piece, acc_piece, count):
        whole_block = lax.dynamic_index_in_dim(tiles, piece_index, 0, keepdims=False)
        block = whole_block.reshape(planes * count, tile_len)
        feat_flat = feat_piece.reshape(planes * count, width)
        query_term = lax.dot_general(
            block, feat_flat, (((0,), (0,)), ((), ())), preferred_element_type=jnp.float32
        )
        acc_new = acc_piece + jnp.dot(
            block, query_feats, preferred_element_type=jnp.float32
        ).reshape(planes, count, width)
        return (query_term, acc_new)

    query_start = jnp.zeros((tile_len, width), jnp.float32)

    def turn_one(turn_index, carry):
        query_total, feat_piece, acc_piece = carry
        term_piece, acc_piece = project(
            (own_index - turn_index) % cycle_size, feat_piece, acc_piece, columns
        )
        feat_piece = shifted(feat_piece, "blk", 1)
        acc_piece = shifted(acc_piece, "blk", 1)
        return (query_total + term_piece, feat_piece, acc_piece)

    start = (query_start, support_feats, jnp.zeros((planes, columns, width), jnp.float32))
    query_total, feat_piece, support_total = lax.fori_loop(0, cycle_size, turn_one, start)
    query_grad = (
        lax.psum_scatter(query_total, ("sub", "pair"), scatter_dimension=0, tiled=True)
        * scale_factor
    )
    return (query_grad, support_total * scale_factor)


def split_taps(kernel):
    high = lax.reduce_precision(kernel, 8, 7)
    return high, kernel - high


def banded(taps, step):
    total = jnp.where(step == 1, taps[2], 0.0)
    return jnp.where(step == 0, taps[1], jnp.where(step == -1, taps[0], total))


def matrix_kernel(count, columns, place_ref, taps_ref, t_ref, rim_ref, wh_ref, wl_ref):
    cells = count * columns

    def taps(part, kernel, a, b):
        return taps_ref[((part * 2 + kernel) * 3 + a) * 3 + b]

    def span(shape, dim):
        return lax.broadcasted_iota(jnp.int32, shape, dim)

    square = (QW, QW)
    step = span(square, 0) - span(square, 1)
    for part, w_ref in enumerate((wh_ref, wl_ref)):
        bands = [
            banded([taps(part, 0, a, b) for b in range(3)], step).astype(jnp.bfloat16)
            for a in range(3)
        ]
        for source in range(4):
            for target in range(2):
                a = source - target
                block = bands[a] if 0 <= a <= 2 else jnp.zeros(square, jnp.bfloat16)
                w_ref[source * QW : (source + 1) * QW, target * QW : (target + 1) * QW] = block
    group = 4 * columns
    shape = (2 * columns, group)
    row_step = span(shape, 1) // columns - span(shape, 0) // columns - 1
    col_step = lax.rem(span(shape, 1), columns) - lax.rem(span(shape, 0), columns)
    beside = jnp.where(place_ref[1] == 0, columns, -1)
    rim_shape = (cells, rim_ref.shape[1] // 2)
    rim_row = span(rim_shape, 1) - span(rim_shape, 0) // columns
    rim_col = beside - lax.rem(span(rim_shape, 0), columns)
    for part in range(2):
        rows = [
            banded([taps(part, 1, a, b) for a in range(3)], row_step) for b in range(3)
        ]
        block = banded(rows, col_step).astype(jnp.bfloat16)
        t_ref[part * 2 * columns : (part + 1) * 2 * columns, :] = block
        rows = [banded([taps(part, 1, a, b) for a in range(3)], rim_row) for b in range(3)]
        block = banded(rows, rim_col).astype(jnp.bfloat16)
        rim_ref[:, part * rim_shape[1] : (part + 1) * rim_shape[1]] = block


def matrix_call(place, query_kernel, support_kernel, count, columns, edge):
    query_parts = split_taps(query_kernel)
    support_parts = split_taps(support_kernel)
    taps = jnp.stack(
        [query_parts[0], support_parts[0], query_parts[1], support_parts[1]]
    ).reshape(-1)
    shapes = [
        (4 * columns, 4 * columns),
        (count * columns, 2 * edge),
        (4 * QW, 2 * QW),
        (4 * QW, 2 * QW),
    ]
    return pl.pallas_call(
        lambda *refs: matrix_kernel(count, columns, *refs),
        out_shape=[jax.ShapeDtypeStruct(shape, jnp.bfloat16) for shape in shapes],
        in_specs=[pl.BlockSpec(memory_space=pltpu.SMEM)] * 2,
        out_specs=[pl.BlockSpec(memory_space=pltpu.VMEM)] * 4,
        cost_estimate=pl.CostEstimate(
            flops=20 * QW * QW * count, bytes_accessed=32 * QW * QW, transcendentals=0
        ),
        compiler_params=pltpu.CompilerParams(vmem_limit_bytes=4 << 20),
        name="matrix_kernel",
    )(place, taps)


def gather_kernel(count, columns, tile, place_ref, *refs):
    pieces, cells_ref, rim_ref = refs[:count], refs[count], refs[count + 1]
    own = place_ref[0]
    first = place_ref[1] != 0
    inner = slice(QW, QW + tile)
    empty = jnp.zeros((columns, tile + 2 * QW), jnp.bfloat16)
    cells_ref[:columns, :] = empty
    cells_ref[(count + 1) * columns :, :] = empty
    edge = rim_ref.shape[0] // 2
    span = lax.broadcasted_iota(jnp.int32, (edge, tile), 0)
    total = jnp.zeros(span.shape, jnp.float32)
    for k, piece in enumerate(reversed(pieces)):
        start = pl.multiple_of(((own ^ k) + 1) * columns, columns)
        cells_ref[pl.ds(start, columns), :] = piece[:, : tile + 2 * QW]
        head = piece[:16, inner].astype(jnp.float32)[:1]
        tail = piece[columns - 16 :, inner].astype(jnp.float32)[15:]
        row = jnp.where(first, head, tail)
        total = jnp.where(span == (own ^ k), row, total)
    rim_ref[:edge, :] = total.astype(jnp.bfloat16)
    rim_ref[edge:, :] = total.astype(jnp.bfloat16)


def gather_call(place, pieces, tile, edge):
    count = len(pieces)
    columns, reach = pieces[0].shape
    return pl.pallas_call(
        lambda *refs: gather_kernel(count, columns, tile, *refs),
        out_shape=[
            jax.ShapeDtypeStruct(((count + 2) * columns, reach), jnp.bfloat16),
            jax.ShapeDtypeStruct((2 * edge, tile), jnp.bfloat16),
        ],
        in_specs=[pl.BlockSpec(memory_space=pltpu.SMEM)]
        + [pl.BlockSpec(memory_space=pltpu.VMEM)] * count,
        out_specs=[pl.BlockSpec(memory_space=pltpu.VMEM)] * 2,
        compiler_params=pltpu.CompilerParams(vmem_limit_bytes=4 << 20),
        cost_estimate=pl.CostEstimate(
            flops=count * tile, bytes_accessed=4 * count * columns * reach, transcendentals=0
        ),
        name="gather_kernel",
    )(place, *reversed(pieces))


def product(left, right):
    return jnp.dot(left, right, preferred_element_type=jnp.float32)


def corr_kernel(group, columns, tile, *refs):
    place_ref, cells_ref, rim_ref, t_ref, edge_ref, wh_ref, wl_ref = refs[:7]
    corr_ref = refs[-1]
    move_ref, stay_ref, keep_ref, send_ref = refs[-5:-1]
    half = corr_ref.shape[0] // columns
    own = place_ref[0]
    core = place_ref[1]
    base = ((own // half) ^ group) * half
    rows = half * columns
    pair = 2 * columns

    def plane_rows(plane, size):
        return pl.ds(pl.multiple_of(plane * columns, columns), size)

    step = 2 * QW
    for low in range(0, tile, step):
        window = cells_ref[plane_rows(base + 1, rows), low : low + 2 * step]
        total = product(window, wh_ref[...]) + product(window, wl_ref[...])
        edges = edge_ref[plane_rows(base, rows), :]
        total += product(edges, rim_ref[:, low : low + step])
        for at in range(0, half, 2):
            middle = cells_ref[plane_rows(base + at, 2 * pair), low + QW : low + QW + step]
            both = product(t_ref[...], middle)
            top = at * columns
            block = total[top : top + pair] + both[:pair] + both[pair:]
            corr_ref[top : top + pair, low : low + step] = block.astype(jnp.bfloat16)
    width = tile // 2
    for k in range(half):
        source = plane_rows(lax.rem(own, half) ^ k, columns)
        out_ref = move_ref if k % 2 else stay_ref
        out_ref[k // 2 * columns : (k // 2 + 1) * columns, :] = corr_ref[source, :]
        for half_ref, which in ((keep_ref, core), (send_ref, 1 - core)):
            start = pl.multiple_of(which * width, width)
            half_ref[k * columns : (k + 1) * columns, :] = corr_ref[source, pl.ds(start, width)]
    for earlier_ref, half_ref in zip(refs[7:-5], (keep_ref, send_ref)):
        half_ref[rows:, :] = earlier_ref[...]


def corr_call(group, place, cells, rim, mats, count, earlier=()):
    tile = rim.shape[1]
    columns = cells.shape[0] // (count + 2)
    half = count // 2
    rows = half * columns
    vmem = pl.BlockSpec(memory_space=pltpu.VMEM)
    wide = jax.ShapeDtypeStruct((rows // 2, tile), jnp.bfloat16)
    tall = jax.ShapeDtypeStruct((2 * rows if earlier else rows, tile // 2), jnp.bfloat16)
    return pl.pallas_call(
        lambda *refs: corr_kernel(group, columns, tile, *refs),
        out_shape=[wide, wide, tall, tall],
        in_specs=[pl.BlockSpec(memory_space=pltpu.SMEM)] + [vmem] * (6 + len(earlier)),
        out_specs=[vmem] * 4,
        scratch_shapes=[pltpu.VMEM((rows, tile), jnp.bfloat16)],
        compiler_params=pltpu.CompilerParams(vmem_limit_bytes=6 << 20),
        cost_estimate=pl.CostEstimate(
            flops=2 * rows * tile * (8 * columns + 8 * QW),
            bytes_accessed=8 * rows * tile,
            transcendentals=0,
        ),
        name="corr_kernel",
    )(place, cells, rim, *mats, *earlier)


def partial_kernel(columns, stay_ref, moved_ref, here_ref, there_ref, *outs):
    width = here_ref.shape[1]
    step = 2 * QW
    for low in range(0, width, step):
        lanes = slice(low, low + step)
        total = product(stay_ref[...], here_ref[:, lanes])
        total += product(moved_ref[...], there_ref[:, lanes])
        for k, out_ref in enumerate(outs):
            out_ref[:, lanes] = total[k * columns : (k + 1) * columns].astype(out_ref.dtype)


def partial_call(stay, moved, here, there, columns, types):
    rows, tile = stay.shape
    width = here.shape[1]
    vmem = pl.BlockSpec(memory_space=pltpu.VMEM)
    return pl.pallas_call(
        lambda *refs: partial_kernel(columns, *refs),
        out_shape=[jax.ShapeDtypeStruct((columns, width), kind) for kind in types],
        in_specs=[vmem] * 4,
        out_specs=[vmem] * len(types),
        compiler_params=pltpu.CompilerParams(vmem_limit_bytes=6 << 20),
        cost_estimate=pl.CostEstimate(
            flops=4 * rows * tile * width, bytes_accessed=4 * tile * width, transcendentals=0
        ),
        name="partial_kernel",
    )(stay, moved, here, there)


def stack_call(blocks):
    columns, width = blocks[0].shape

    def kernel(*refs):
        for k in range(len(blocks)):
            refs[-1][k * columns : (k + 1) * columns, :] = refs[k][...]

    vmem = pl.BlockSpec(memory_space=pltpu.VMEM)
    return pl.pallas_call(
        kernel,
        out_shape=jax.ShapeDtypeStruct((len(blocks) * columns, width), jnp.bfloat16),
        in_specs=[vmem] * len(blocks),
        out_specs=vmem,
        compiler_params=pltpu.CompilerParams(vmem_limit_bytes=4 << 20),
        cost_estimate=pl.CostEstimate(
            flops=0, bytes_accessed=4 * len(blocks) * columns * width, transcendentals=0
        ),
        name="stack_kernel",
    )(*blocks)


def tile_shards(grad_volume, query_feats, support_feats, query_kernel, support_kernel):
    _, columns, queries = grad_volume.shape
    width = query_feats.shape[1]
    outer = lax.axis_size("blk")
    inner = lax.axis_size("sub")
    count = outer * inner
    half = count // 2
    tile = queries // count
    scale_factor = 1.0 / math.sqrt(width)
    own = lax.axis_index(("blk", "sub"))
    side = lax.axis_index("sub")
    core = lax.axis_index("pair")
    place = jnp.stack([own, core]).astype(jnp.int32)

    def exchanged(value, mask):
        return lax.ppermute(value, ("blk", "sub"), [(i, i ^ mask) for i in range(count)])

    def swapped(value):
        return lax.ppermute(value, "pair", [(0, 1), (1, 0)])

    volume = jnp.pad(grad_volume[0], ((0, 0), (QW, QW)))

    def piece(mask):
        return lax.dynamic_slice(volume, (0, (own ^ mask) * tile), (columns, tile + 2 * QW))

    reach = tile + 2 * QW
    feats = support_feats[0]
    merged = []
    pieces = [piece(mask) for mask in range(count)]
    held = [feats] + [None] * (count - 1)
    for mask in range(count - 1, 0, -1):
        if mask in merged:
            both = exchanged(jnp.concatenate([pieces[mask], feats], axis=1), mask)
            pieces[mask] = both
            held[mask] = both[:, reach:]
        else:
            pieces[mask] = exchanged(pieces[mask], mask)
    bit = half
    while bit:
        for k in range(0, count, 2 * bit):
            if held[k ^ bit] is None:
                held[k ^ bit] = exchanged(held[k], bit)
        bit //= 2

    edge = 16 * -(-count // 16)
    mats = matrix_call(place, query_kernel, support_kernel, count, columns, edge)
    here = lax.dynamic_slice(query_feats, (side * tile, 0), (tile, width))
    there = lax.dynamic_slice(query_feats, ((side ^ 1) * tile, 0), (tile, width))
    ordered = held + [pieces[k] for k in [5, 4, 3, 2, 1, 7, 6, 0]]
    ordered, mats, here, there = lax.optimization_barrier((ordered, mats, here, there))
    held, landed = ordered[:count], ordered[count:]
    for at, k in enumerate([5, 4, 3, 2, 1, 7, 6, 0]):
        pieces[k] = landed[at]
    cells, rim = gather_call(place, pieces, tile, edge)
    rim = swapped(rim)
    feats = stack_call(held)
    across = swapped(feats)
    move1, stay1, keep, send = corr_call(1, place, cells, rim, mats, count)
    moved1 = exchanged(move1, 1)
    move0, stay0, keep, send = corr_call(0, place, cells, rim, mats, count, (keep, send))
    moved0 = exchanged(move0, 1)
    other = swapped(send)
    narrow = [jnp.bfloat16] * (count // 4)
    parts1 = partial_call(stay1, moved1, here, there, columns, narrow)
    parts0 = partial_call(stay0, moved0, here, there, columns, [jnp.float32] + narrow[1:])
    landed = [exchanged(part, half + 2 * at) for at, part in enumerate(parts1)]
    landed += [exchanged(part, 2 * at) for at, part in enumerate(parts0) if at]

    def query_term(block, feats):
        return lax.dot_general(
            block, feats, (((0,), (0,)), ((), ())), preferred_element_type=jnp.float32
        )

    rows = half * columns
    query_grad = query_term(keep[:rows], feats[:rows]) + query_term(keep[rows:], feats[rows:])
    query_grad += query_term(other[:rows], across[:rows]) + query_term(other[rows:], across[rows:])
    query_grad *= scale_factor
    landed[0], query_grad = lax.optimization_barrier((landed[0], query_grad))
    support_grad = parts0[0]
    for term in landed:
        support_grad = support_grad + term.astype(jnp.float32)
    return (query_grad, (support_grad * scale_factor)[None])


def tiles_fit(mesh, grad_volume):
    shape = dict(mesh.shape)
    count = shape["blk"] * shape["sub"]
    planes = grad_volume.shape[0] // (shape["grp"] * count)
    columns = grad_volume.shape[1] // shape["pair"]
    return (
        planes == 1
        and shape["pair"] == 2
        and shape["sub"] == 2
        and count >= 4
        and count & (count - 1) == 0
        and count * columns <= 1024
        and columns % 16 == 0
        and QW % columns == 0
        and count * columns % QW == 0
        and QH * QW % (count * 2 * QW) == 0
    )


def solution(mesh):
    in_specs = (
        P(("grp", "blk", "sub"), "pair", None),
        P(("grp", "blk"), None),
        P(("grp", "blk", "sub"), "pair", None),
        P(),
        P(),
    )
    out_specs = (P(("grp", "blk", "sub", "pair"), None), P(("grp", "blk", "sub"), "pair", None))

    def program(grad_volume, *rest):
        body = tile_shards if tiles_fit(mesh, grad_volume) else ring_shards
        mapped = jax.shard_map(
            body, mesh=mesh, in_specs=in_specs, out_specs=out_specs, check_vma=False
        )
        return mapped(grad_volume, *rest)

    return program
```

```python
import math

import jax
import jax.numpy as jnp
from jax import lax
from jax.experimental import pallas as pl
from jax.experimental.pallas import tpu as pltpu
from jax.sharding import PartitionSpec as P

QW = 128
QH = 64


def extended(cells, sides, width):
    for axis, dim in sides:
        count = lax.axis_size(axis)
        ends = count - 1
        head = lax.slice_in_dim(cells, 0, width, axis=dim)
        tail = lax.slice_in_dim(cells, cells.shape[dim] - width, cells.shape[dim], axis=dim)
        cells = jnp.concatenate(
            [
                lax.ppermute(tail, axis, [(i, (i + 1) % count) for i in range(ends)]),
                cells,
                lax.ppermute(head, axis, [((i + 1) % count, i) for i in range(ends)]),
            ],
            axis=dim,
        )
    return cells


def shifted(value, axis, steps):
    count = lax.axis_size(axis)
    pairs = [(source, (source + steps) % count) for source in range(count)]
    return lax.ppermute(value, axis, pairs)


def query_pass(volume, kernel):
    planes, columns, queries = volume.shape
    grid = volume.astype(jnp.float32).reshape(planes, columns, QH, QW)
    padded = jnp.pad(grid, ((0, 0), (0, 0), (1, 1), (1, 1)))
    total = jnp.zeros_like(grid)
    for row_shift in range(3):
        for col_shift in range(3):
            total = (
                total
                + kernel[row_shift, col_shift]
                * padded[:, :, row_shift : row_shift + QH, col_shift : col_shift + QW]
            )
    return total.reshape(planes, columns, queries)


def support_pass(rimmed, kernel, planes, columns):
    total = jnp.zeros((planes, columns, rimmed.shape[2]), jnp.float32)
    for row_shift in range(3):
        for col_shift in range(3):
            total = total + kernel[row_shift, col_shift] * rimmed[
                row_shift : row_shift + planes, col_shift : col_shift + columns
            ].astype(jnp.float32)
    return total


def ring_shards(grad_volume, query_feats, support_feats, query_kernel, support_kernel):
    planes, columns, queries = grad_volume.shape
    rimmed = extended(grad_volume, ((("blk", "sub"), 0), ("pair", 1)), 1)
    corr_grad = (
        query_pass(grad_volume, query_kernel)
        + support_pass(rimmed, support_kernel, planes, columns)
    ).astype(jnp.bfloat16)
    moved = lax.all_to_all(corr_grad, "blk", split_axis=2, concat_axis=0, tiled=True)
    cycle_size = lax.axis_size("blk")
    own_index = lax.axis_index("blk")
    tile_len = moved.shape[2]
    tiles = moved.reshape(cycle_size, planes, columns, tile_len)
    width = query_feats.shape[1]
    scale_factor = 1.0 / math.sqrt(width)

    def project(piece_index, feat_piece, acc_piece, count):
        whole_block = lax.dynamic_index_in_dim(tiles, piece_index, 0, keepdims=False)
        block = whole_block.reshape(planes * count, tile_len)
        feat_flat = feat_piece.reshape(planes * count, width)
        query_term = lax.dot_general(
            block, feat_flat, (((0,), (0,)), ((), ())), preferred_element_type=jnp.float32
        )
        acc_new = acc_piece + jnp.dot(
            block, query_feats, preferred_element_type=jnp.float32
        ).reshape(planes, count, width)
        return (query_term, acc_new)

    query_start = jnp.zeros((tile_len, width), jnp.float32)

    def turn_one(turn_index, carry):
        query_total, feat_piece, acc_piece = carry
        term_piece, acc_piece = project(
            (own_index - turn_index) % cycle_size, feat_piece, acc_piece, columns
        )
        feat_piece = shifted(feat_piece, "blk", 1)
        acc_piece = shifted(acc_piece, "blk", 1)
        return (query_total + term_piece, feat_piece, acc_piece)

    start = (query_start, support_feats, jnp.zeros((planes, columns, width), jnp.float32))
    query_total, feat_piece, support_total = lax.fori_loop(0, cycle_size, turn_one, start)
    query_grad = (
        lax.psum_scatter(query_total, ("sub", "pair"), scatter_dimension=0, tiled=True)
        * scale_factor
    )
    return (query_grad, support_total * scale_factor)


def split_taps(kernel):
    high = lax.reduce_precision(kernel, 8, 7)
    return high, kernel - high


def banded(taps, step):
    total = jnp.where(step == 1, taps[2], 0.0)
    return jnp.where(step == 0, taps[1], jnp.where(step == -1, taps[0], total))


def matrix_kernel(count, columns, place_ref, taps_ref, t_ref, rim_ref, wh_ref, wl_ref):
    cells = count * columns

    def taps(part, kernel, a, b):
        return taps_ref[((part * 2 + kernel) * 3 + a) * 3 + b]

    def span(shape, dim):
        return lax.broadcasted_iota(jnp.int32, shape, dim)

    square = (QW, QW)
    step = span(square, 0) - span(square, 1)
    for part, w_ref in enumerate((wh_ref, wl_ref)):
        bands = [
            banded([taps(part, 0, a, b) for b in range(3)], step).astype(jnp.bfloat16)
            for a in range(3)
        ]
        for source in range(4):
            for target in range(2):
                a = source - target
                block = bands[a] if 0 <= a <= 2 else jnp.zeros(square, jnp.bfloat16)
                w_ref[source * QW : (source + 1) * QW, target * QW : (target + 1) * QW] = block
    group = 4 * columns
    shape = (2 * columns, group)
    row_step = span(shape, 1) // columns - span(shape, 0) // columns - 1
    col_step = lax.rem(span(shape, 1), columns) - lax.rem(span(shape, 0), columns)
    beside = jnp.where(place_ref[1] == 0, columns, -1)
    rim_shape = (cells, rim_ref.shape[1] // 2)
    rim_row = span(rim_shape, 1) - span(rim_shape, 0) // columns
    rim_col = beside - lax.rem(span(rim_shape, 0), columns)
    for part in range(2):
        rows = [
            banded([taps(part, 1, a, b) for a in range(3)], row_step) for b in range(3)
        ]
        block = banded(rows, col_step).astype(jnp.bfloat16)
        t_ref[part * 2 * columns : (part + 1) * 2 * columns, :] = block
        rows = [banded([taps(part, 1, a, b) for a in range(3)], rim_row) for b in range(3)]
        block = banded(rows, rim_col).astype(jnp.bfloat16)
        rim_ref[:, part * rim_shape[1] : (part + 1) * rim_shape[1]] = block


def matrix_call(place, query_kernel, support_kernel, count, columns, edge):
    query_parts = split_taps(query_kernel)
    support_parts = split_taps(support_kernel)
    taps = jnp.stack(
        [query_parts[0], support_parts[0], query_parts[1], support_parts[1]]
    ).reshape(-1)
    shapes = [
        (4 * columns, 4 * columns),
        (count * columns, 2 * edge),
        (4 * QW, 2 * QW),
        (4 * QW, 2 * QW),
    ]
    return pl.pallas_call(
        lambda *refs: matrix_kernel(count, columns, *refs),
        out_shape=[jax.ShapeDtypeStruct(shape, jnp.bfloat16) for shape in shapes],
        in_specs=[pl.BlockSpec(memory_space=pltpu.SMEM)] * 2,
        out_specs=[pl.BlockSpec(memory_space=pltpu.VMEM)] * 4,
        cost_estimate=pl.CostEstimate(
            flops=20 * QW * QW * count, bytes_accessed=32 * QW * QW, transcendentals=0
        ),
        compiler_params=pltpu.CompilerParams(vmem_limit_bytes=4 << 20),
        name="matrix_kernel",
    )(place, taps)


def gather_kernel(count, columns, tile, place_ref, *refs):
    pieces, cells_ref, rim_ref = refs[:count], refs[count], refs[count + 1]
    own = place_ref[0]
    first = place_ref[1] != 0
    inner = slice(QW, QW + tile)
    empty = jnp.zeros((columns, tile + 2 * QW), jnp.bfloat16)
    cells_ref[:columns, :] = empty
    cells_ref[(count + 1) * columns :, :] = empty
    edge = rim_ref.shape[0] // 2
    span = lax.broadcasted_iota(jnp.int32, (edge, tile), 0)
    total = jnp.zeros(span.shape, jnp.float32)
    for k, piece in enumerate(reversed(pieces)):
        start = pl.multiple_of(((own ^ k) + 1) * columns, columns)
        cells_ref[pl.ds(start, columns), :] = piece[:, : tile + 2 * QW]
        head = piece[:16, inner].astype(jnp.float32)[:1]
        tail = piece[columns - 16 :, inner].astype(jnp.float32)[15:]
        row = jnp.where(first, head, tail)
        total = jnp.where(span == (own ^ k), row, total)
    rim_ref[:edge, :] = total.astype(jnp.bfloat16)
    rim_ref[edge:, :] = total.astype(jnp.bfloat16)


def gather_call(place, pieces, tile, edge):
    count = len(pieces)
    columns, reach = pieces[0].shape
    return pl.pallas_call(
        lambda *refs: gather_kernel(count, columns, tile, *refs),
        out_shape=[
            jax.ShapeDtypeStruct(((count + 2) * columns, reach), jnp.bfloat16),
            jax.ShapeDtypeStruct((2 * edge, tile), jnp.bfloat16),
        ],
        in_specs=[pl.BlockSpec(memory_space=pltpu.SMEM)]
        + [pl.BlockSpec(memory_space=pltpu.VMEM)] * count,
        out_specs=[pl.BlockSpec(memory_space=pltpu.VMEM)] * 2,
        compiler_params=pltpu.CompilerParams(vmem_limit_bytes=4 << 20),
        cost_estimate=pl.CostEstimate(
            flops=count * tile, bytes_accessed=4 * count * columns * reach, transcendentals=0
        ),
        name="gather_kernel",
    )(place, *reversed(pieces))


def product(left, right):
    return jnp.dot(left, right, preferred_element_type=jnp.float32)


def query_kernel(columns, tile, cells_ref, wh_ref, wl_ref, out_ref):
    rows = out_ref.shape[0]
    step = 2 * QW
    for low in range(0, tile, step):
        window = cells_ref[columns : columns + rows, low : low + 2 * step]
        total = product(window, wh_ref[...]) + product(window, wl_ref[...])
        out_ref[:, low : low + step] = total


def query_call(cells, high, low, columns, tile):
    rows = cells.shape[0] - 2 * columns
    return pl.pallas_call(
        lambda *refs: query_kernel(columns, tile, *refs),
        out_shape=jax.ShapeDtypeStruct((rows, tile), jnp.float32),
        in_specs=[pl.BlockSpec(memory_space=pltpu.VMEM)] * 3,
        out_specs=pl.BlockSpec(memory_space=pltpu.VMEM),
        compiler_params=pltpu.CompilerParams(vmem_limit_bytes=6 << 20),
        cost_estimate=pl.CostEstimate(
            flops=16 * rows * tile * QW, bytes_accessed=8 * rows * tile, transcendentals=0
        ),
        name="query_kernel",
    )(cells, high, low)


def corr_kernel(group, columns, tile, *refs):
    place_ref, cells_ref, rim_ref, t_ref, edge_ref, query_ref = refs[:6]
    corr_ref = refs[-1]
    move_ref, stay_ref, keep_ref, send_ref = refs[-5:-1]
    half = corr_ref.shape[0] // columns
    own = place_ref[0]
    core = place_ref[1]
    base = ((own // half) ^ group) * half
    rows = half * columns
    pair = 2 * columns

    def plane_rows(plane, size):
        return pl.ds(pl.multiple_of(plane * columns, columns), size)

    step = 2 * QW
    for low in range(0, tile, step):
        total = query_ref[plane_rows(base, rows), low : low + step]
        edges = edge_ref[plane_rows(base, rows), :]
        total += product(edges, rim_ref[:, low : low + step])
        for at in range(0, half, 2):
            middle = cells_ref[plane_rows(base + at, 2 * pair), low + QW : low + QW + step]
            both = product(t_ref[...], middle)
            top = at * columns
            block = total[top : top + pair] + both[:pair] + both[pair:]
            corr_ref[top : top + pair, low : low + step] = block.astype(jnp.bfloat16)
    width = tile // 2
    for k in range(half):
        source = plane_rows(lax.rem(own, half) ^ k, columns)
        out_ref = move_ref if k % 2 else stay_ref
        out_ref[k // 2 * columns : (k // 2 + 1) * columns, :] = corr_ref[source, :]
        for half_ref, which in ((keep_ref, core), (send_ref, 1 - core)):
            start = pl.multiple_of(which * width, width)
            half_ref[k * columns : (k + 1) * columns, :] = corr_ref[source, pl.ds(start, width)]
    for earlier_ref, half_ref in zip(refs[6:-5], (keep_ref, send_ref)):
        half_ref[rows:, :] = earlier_ref[...]


def corr_call(group, place, cells, rim, mats, count, earlier=()):
    tile = rim.shape[1]
    columns = cells.shape[0] // (count + 2)
    half = count // 2
    rows = half * columns
    vmem = pl.BlockSpec(memory_space=pltpu.VMEM)
    wide = jax.ShapeDtypeStruct((rows // 2, tile), jnp.bfloat16)
    tall = jax.ShapeDtypeStruct((2 * rows if earlier else rows, tile // 2), jnp.bfloat16)
    return pl.pallas_call(
        lambda *refs: corr_kernel(group, columns, tile, *refs),
        out_shape=[wide, wide, tall, tall],
        in_specs=[pl.BlockSpec(memory_space=pltpu.SMEM)] + [vmem] * (5 + len(earlier)),
        out_specs=[vmem] * 4,
        scratch_shapes=[pltpu.VMEM((rows, tile), jnp.bfloat16)],
        compiler_params=pltpu.CompilerParams(vmem_limit_bytes=6 << 20),
        cost_estimate=pl.CostEstimate(
            flops=2 * rows * tile * 8 * columns,
            bytes_accessed=8 * rows * tile,
            transcendentals=0,
        ),
        name="corr_kernel",
    )(place, cells, rim, *mats, *earlier)


def partial_kernel(columns, stay_ref, moved_ref, here_ref, there_ref, *outs):
    width = here_ref.shape[1]
    step = 2 * QW
    for low in range(0, width, step):
        lanes = slice(low, low + step)
        total = product(stay_ref[...], here_ref[:, lanes])
        total += product(moved_ref[...], there_ref[:, lanes])
        for k, out_ref in enumerate(outs):
            out_ref[:, lanes] = total[k * columns : (k + 1) * columns].astype(out_ref.dtype)


def partial_call(stay, moved, here, there, columns, types):
    rows, tile = stay.shape
    width = here.shape[1]
    vmem = pl.BlockSpec(memory_space=pltpu.VMEM)
    return pl.pallas_call(
        lambda *refs: partial_kernel(columns, *refs),
        out_shape=[jax.ShapeDtypeStruct((columns, width), kind) for kind in types],
        in_specs=[vmem] * 4,
        out_specs=[vmem] * len(types),
        compiler_params=pltpu.CompilerParams(vmem_limit_bytes=6 << 20),
        cost_estimate=pl.CostEstimate(
            flops=4 * rows * tile * width, bytes_accessed=4 * tile * width, transcendentals=0
        ),
        name="partial_kernel",
    )(stay, moved, here, there)


def stack_call(blocks):
    columns, width = blocks[0].shape

    def kernel(*refs):
        for k in range(len(blocks)):
            refs[-1][k * columns : (k + 1) * columns, :] = refs[k][...]

    vmem = pl.BlockSpec(memory_space=pltpu.VMEM)
    return pl.pallas_call(
        kernel,
        out_shape=jax.ShapeDtypeStruct((len(blocks) * columns, width), jnp.bfloat16),
        in_specs=[vmem] * len(blocks),
        out_specs=vmem,
        compiler_params=pltpu.CompilerParams(vmem_limit_bytes=4 << 20),
        cost_estimate=pl.CostEstimate(
            flops=0, bytes_accessed=4 * len(blocks) * columns * width, transcendentals=0
        ),
        name="stack_kernel",
    )(*blocks)


def tile_shards(grad_volume, query_feats, support_feats, query_kernel, support_kernel):
    _, columns, queries = grad_volume.shape
    width = query_feats.shape[1]
    outer = lax.axis_size("blk")
    inner = lax.axis_size("sub")
    count = outer * inner
    half = count // 2
    tile = queries // count
    scale_factor = 1.0 / math.sqrt(width)
    own = lax.axis_index(("blk", "sub"))
    side = lax.axis_index("sub")
    core = lax.axis_index("pair")
    place = jnp.stack([own, core]).astype(jnp.int32)

    def exchanged(value, mask):
        return lax.ppermute(value, ("blk", "sub"), [(i, i ^ mask) for i in range(count)])

    def swapped(value):
        return lax.ppermute(value, "pair", [(0, 1), (1, 0)])

    volume = jnp.pad(grad_volume[0], ((0, 0), (QW, QW)))

    def piece(mask):
        return lax.dynamic_slice(volume, (0, (own ^ mask) * tile), (columns, tile + 2 * QW))

    reach = tile + 2 * QW
    feats = support_feats[0]
    merged = []
    pieces = [piece(mask) for mask in range(count)]
    held = [feats] + [None] * (count - 1)
    for mask in range(count - 1, 0, -1):
        if mask in merged:
            both = exchanged(jnp.concatenate([pieces[mask], feats], axis=1), mask)
            pieces[mask] = both
            held[mask] = both[:, reach:]
        else:
            pieces[mask] = exchanged(pieces[mask], mask)
    bit = half
    while bit:
        for k in range(0, count, 2 * bit):
            if held[k ^ bit] is None:
                held[k ^ bit] = exchanged(held[k], bit)
        bit //= 2

    edge = 16 * -(-count // 16)
    mats = matrix_call(place, query_kernel, support_kernel, count, columns, edge)
    here = lax.dynamic_slice(query_feats, (side * tile, 0), (tile, width))
    there = lax.dynamic_slice(query_feats, ((side ^ 1) * tile, 0), (tile, width))
    ordered = held + [pieces[k] for k in [7, 6, 5, 4, 3, 2, 1, 0]]
    ordered, mats, here, there = lax.optimization_barrier((ordered, mats, here, there))
    held, landed = ordered[:count], ordered[count:]
    for at, k in enumerate([7, 6, 5, 4, 3, 2, 1, 0]):
        pieces[k] = landed[at]
    cells, rim = gather_call(place, pieces, tile, edge)
    rim = swapped(rim)
    mats = [mats[0], mats[1], query_call(cells, mats[2], mats[3], columns, tile)]
    feats = stack_call(held)
    across = swapped(feats)
    move1, stay1, keep, send = corr_call(1, place, cells, rim, mats, count)
    moved1 = exchanged(move1, 1)
    move0, stay0, keep, send = corr_call(0, place, cells, rim, mats, count, (keep, send))
    moved0 = exchanged(move0, 1)
    other = swapped(send)
    narrow = [jnp.bfloat16] * (count // 4)
    parts1 = partial_call(stay1, moved1, here, there, columns, narrow)
    parts0 = partial_call(stay0, moved0, here, there, columns, [jnp.float32] + narrow[1:])
    landed = [exchanged(part, half + 2 * at) for at, part in enumerate(parts1)]
    landed += [exchanged(part, 2 * at) for at, part in enumerate(parts0) if at]

    def query_term(block, feats):
        return lax.dot_general(
            block, feats, (((0,), (0,)), ((), ())), preferred_element_type=jnp.float32
        )

    rows = half * columns
    query_grad = query_term(keep[:rows], feats[:rows]) + query_term(keep[rows:], feats[rows:])
    query_grad += query_term(other[:rows], across[:rows]) + query_term(other[rows:], across[rows:])
    query_grad *= scale_factor
    landed[-1], query_grad = lax.optimization_barrier((landed[-1], query_grad))
    support_grad = parts0[0]
    for term in landed:
        support_grad = support_grad + term.astype(jnp.float32)
    return (query_grad, (support_grad * scale_factor)[None])


def tiles_fit(mesh, grad_volume):
    shape = dict(mesh.shape)
    count = shape["blk"] * shape["sub"]
    planes = grad_volume.shape[0] // (shape["grp"] * count)
    columns = grad_volume.shape[1] // shape["pair"]
    return (
        planes == 1
        and shape["pair"] == 2
        and shape["sub"] == 2
        and count >= 4
        and count & (count - 1) == 0
        and count * columns <= 1024
        and columns % 16 == 0
        and QW % columns == 0
        and count * columns % QW == 0
        and QH * QW % (count * 2 * QW) == 0
    )


def solution(mesh):
    in_specs = (
        P(("grp", "blk", "sub"), "pair", None),
        P(("grp", "blk"), None),
        P(("grp", "blk", "sub"), "pair", None),
        P(),
        P(),
    )
    out_specs = (P(("grp", "blk", "sub", "pair"), None), P(("grp", "blk", "sub"), "pair", None))

    def program(grad_volume, *rest):
        body = tile_shards if tiles_fit(mesh, grad_volume) else ring_shards
        mapped = jax.shard_map(
            body, mesh=mesh, in_specs=in_specs, out_specs=out_specs, check_vma=False
        )
        return mapped(grad_volume, *rest)

    return program
```

```python
import math

import jax
import jax.numpy as jnp
from jax import lax
from jax.experimental import pallas as pl
from jax.experimental.pallas import tpu as pltpu
from jax.sharding import PartitionSpec as P

QW = 128
QH = 64


def extended(cells, sides, width):
    for axis, dim in sides:
        count = lax.axis_size(axis)
        ends = count - 1
        head = lax.slice_in_dim(cells, 0, width, axis=dim)
        tail = lax.slice_in_dim(cells, cells.shape[dim] - width, cells.shape[dim], axis=dim)
        cells = jnp.concatenate(
            [
                lax.ppermute(tail, axis, [(i, (i + 1) % count) for i in range(ends)]),
                cells,
                lax.ppermute(head, axis, [((i + 1) % count, i) for i in range(ends)]),
            ],
            axis=dim,
        )
    return cells


def shifted(value, axis, steps):
    count = lax.axis_size(axis)
    pairs = [(source, (source + steps) % count) for source in range(count)]
    return lax.ppermute(value, axis, pairs)


def query_pass(volume, kernel):
    planes, columns, queries = volume.shape
    grid = volume.astype(jnp.float32).reshape(planes, columns, QH, QW)
    padded = jnp.pad(grid, ((0, 0), (0, 0), (1, 1), (1, 1)))
    total = jnp.zeros_like(grid)
    for row_shift in range(3):
        for col_shift in range(3):
            total = (
                total
                + kernel[row_shift, col_shift]
                * padded[:, :, row_shift : row_shift + QH, col_shift : col_shift + QW]
            )
    return total.reshape(planes, columns, queries)


def support_pass(rimmed, kernel, planes, columns):
    total = jnp.zeros((planes, columns, rimmed.shape[2]), jnp.float32)
    for row_shift in range(3):
        for col_shift in range(3):
            total = total + kernel[row_shift, col_shift] * rimmed[
                row_shift : row_shift + planes, col_shift : col_shift + columns
            ].astype(jnp.float32)
    return total


def ring_shards(grad_volume, query_feats, support_feats, query_kernel, support_kernel):
    planes, columns, queries = grad_volume.shape
    rimmed = extended(grad_volume, ((("blk", "sub"), 0), ("pair", 1)), 1)
    corr_grad = (
        query_pass(grad_volume, query_kernel)
        + support_pass(rimmed, support_kernel, planes, columns)
    ).astype(jnp.bfloat16)
    moved = lax.all_to_all(corr_grad, "blk", split_axis=2, concat_axis=0, tiled=True)
    cycle_size = lax.axis_size("blk")
    own_index = lax.axis_index("blk")
    tile_len = moved.shape[2]
    tiles = moved.reshape(cycle_size, planes, columns, tile_len)
    width = query_feats.shape[1]
    scale_factor = 1.0 / math.sqrt(width)

    def project(piece_index, feat_piece, acc_piece, count):
        whole_block = lax.dynamic_index_in_dim(tiles, piece_index, 0, keepdims=False)
        block = whole_block.reshape(planes * count, tile_len)
        feat_flat = feat_piece.reshape(planes * count, width)
        query_term = lax.dot_general(
            block, feat_flat, (((0,), (0,)), ((), ())), preferred_element_type=jnp.float32
        )
        acc_new = acc_piece + jnp.dot(
            block, query_feats, preferred_element_type=jnp.float32
        ).reshape(planes, count, width)
        return (query_term, acc_new)

    query_start = jnp.zeros((tile_len, width), jnp.float32)

    def turn_one(turn_index, carry):
        query_total, feat_piece, acc_piece = carry
        term_piece, acc_piece = project(
            (own_index - turn_index) % cycle_size, feat_piece, acc_piece, columns
        )
        feat_piece = shifted(feat_piece, "blk", 1)
        acc_piece = shifted(acc_piece, "blk", 1)
        return (query_total + term_piece, feat_piece, acc_piece)

    start = (query_start, support_feats, jnp.zeros((planes, columns, width), jnp.float32))
    query_total, feat_piece, support_total = lax.fori_loop(0, cycle_size, turn_one, start)
    query_grad = (
        lax.psum_scatter(query_total, ("sub", "pair"), scatter_dimension=0, tiled=True)
        * scale_factor
    )
    return (query_grad, support_total * scale_factor)


def split_taps(kernel):
    high = lax.reduce_precision(kernel, 8, 7)
    return high, kernel - high


def banded(taps, step):
    total = jnp.where(step == 1, taps[2], 0.0)
    return jnp.where(step == 0, taps[1], jnp.where(step == -1, taps[0], total))


def matrix_kernel(count, columns, place_ref, taps_ref, t_ref, rim_ref, wh_ref, wl_ref):
    cells = count * columns

    def taps(part, kernel, a, b):
        return taps_ref[((part * 2 + kernel) * 3 + a) * 3 + b]

    def span(shape, dim):
        return lax.broadcasted_iota(jnp.int32, shape, dim)

    square = (QW, QW)
    step = span(square, 0) - span(square, 1)
    for part, w_ref in enumerate((wh_ref, wl_ref)):
        bands = [
            banded([taps(part, 0, a, b) for b in range(3)], step).astype(jnp.bfloat16)
            for a in range(3)
        ]
        for source in range(4):
            for target in range(2):
                a = source - target
                block = bands[a] if 0 <= a <= 2 else jnp.zeros(square, jnp.bfloat16)
                w_ref[source * QW : (source + 1) * QW, target * QW : (target + 1) * QW] = block
    group = 4 * columns
    shape = (2 * columns, group)
    row_step = span(shape, 1) // columns - span(shape, 0) // columns - 1
    col_step = lax.rem(span(shape, 1), columns) - lax.rem(span(shape, 0), columns)
    beside = jnp.where(place_ref[1] == 0, columns, -1)
    rim_shape = (cells, rim_ref.shape[1] // 2)
    rim_row = span(rim_shape, 1) - span(rim_shape, 0) // columns
    rim_col = beside - lax.rem(span(rim_shape, 0), columns)
    for part in range(2):
        rows = [
            banded([taps(part, 1, a, b) for a in range(3)], row_step) for b in range(3)
        ]
        block = banded(rows, col_step).astype(jnp.bfloat16)
        t_ref[part * 2 * columns : (part + 1) * 2 * columns, :] = block
        rows = [banded([taps(part, 1, a, b) for a in range(3)], rim_row) for b in range(3)]
        block = banded(rows, rim_col).astype(jnp.bfloat16)
        rim_ref[:, part * rim_shape[1] : (part + 1) * rim_shape[1]] = block


def matrix_call(place, query_kernel, support_kernel, count, columns, edge):
    query_parts = split_taps(query_kernel)
    support_parts = split_taps(support_kernel)
    taps = jnp.stack(
        [query_parts[0], support_parts[0], query_parts[1], support_parts[1]]
    ).reshape(-1)
    shapes = [
        (4 * columns, 4 * columns),
        (count * columns, 2 * edge),
        (4 * QW, 2 * QW),
        (4 * QW, 2 * QW),
    ]
    return pl.pallas_call(
        lambda *refs: matrix_kernel(count, columns, *refs),
        out_shape=[jax.ShapeDtypeStruct(shape, jnp.bfloat16) for shape in shapes],
        in_specs=[pl.BlockSpec(memory_space=pltpu.SMEM)] * 2,
        out_specs=[pl.BlockSpec(memory_space=pltpu.VMEM)] * 4,
        cost_estimate=pl.CostEstimate(
            flops=20 * QW * QW * count, bytes_accessed=32 * QW * QW, transcendentals=0
        ),
        compiler_params=pltpu.CompilerParams(vmem_limit_bytes=4 << 20),
        name="matrix_kernel",
    )(place, taps)


def gather_kernel(count, columns, tile, place_ref, *refs):
    pieces, cells_ref, rim_ref = refs[:count], refs[count], refs[count + 1]
    own = place_ref[0]
    first = place_ref[1] != 0
    inner = slice(QW, QW + tile)
    empty = jnp.zeros((columns, tile + 2 * QW), jnp.bfloat16)
    cells_ref[:columns, :] = empty
    cells_ref[(count + 1) * columns :, :] = empty
    edge = rim_ref.shape[0] // 2
    span = lax.broadcasted_iota(jnp.int32, (edge, tile), 0)
    total = jnp.zeros(span.shape, jnp.float32)
    for k, piece in enumerate(reversed(pieces)):
        start = pl.multiple_of(((own ^ k) + 1) * columns, columns)
        cells_ref[pl.ds(start, columns), :] = piece[:, : tile + 2 * QW]
        head = piece[:16, inner].astype(jnp.float32)[:1]
        tail = piece[columns - 16 :, inner].astype(jnp.float32)[15:]
        row = jnp.where(first, head, tail)
        total = jnp.where(span == (own ^ k), row, total)
    rim_ref[:edge, :] = total.astype(jnp.bfloat16)
    rim_ref[edge:, :] = total.astype(jnp.bfloat16)


def gather_call(place, pieces, tile, edge):
    count = len(pieces)
    columns, reach = pieces[0].shape
    return pl.pallas_call(
        lambda *refs: gather_kernel(count, columns, tile, *refs),
        out_shape=[
            jax.ShapeDtypeStruct(((count + 2) * columns, reach), jnp.bfloat16),
            jax.ShapeDtypeStruct((2 * edge, tile), jnp.bfloat16),
        ],
        in_specs=[pl.BlockSpec(memory_space=pltpu.SMEM)]
        + [pl.BlockSpec(memory_space=pltpu.VMEM)] * count,
        out_specs=[pl.BlockSpec(memory_space=pltpu.VMEM)] * 2,
        compiler_params=pltpu.CompilerParams(vmem_limit_bytes=4 << 20),
        cost_estimate=pl.CostEstimate(
            flops=count * tile, bytes_accessed=4 * count * columns * reach, transcendentals=0
        ),
        name="gather_kernel",
    )(place, *reversed(pieces))


def product(left, right):
    return jnp.dot(left, right, preferred_element_type=jnp.float32)


def query_kernel(columns, tile, cells_ref, wh_ref, wl_ref, out_ref):
    rows = out_ref.shape[0]
    step = 2 * QW
    for low in range(0, tile, step):
        window = cells_ref[columns : columns + rows, low : low + 2 * step]
        total = product(window, wh_ref[...]) + product(window, wl_ref[...])
        out_ref[:, low : low + step] = total


def query_call(cells, high, low, columns, tile):
    rows = cells.shape[0] - 2 * columns
    return pl.pallas_call(
        lambda *refs: query_kernel(columns, tile, *refs),
        out_shape=jax.ShapeDtypeStruct((rows, tile), jnp.float32),
        in_specs=[pl.BlockSpec(memory_space=pltpu.VMEM)] * 3,
        out_specs=pl.BlockSpec(memory_space=pltpu.VMEM),
        compiler_params=pltpu.CompilerParams(vmem_limit_bytes=6 << 20),
        cost_estimate=pl.CostEstimate(
            flops=16 * rows * tile * QW, bytes_accessed=8 * rows * tile, transcendentals=0
        ),
        name="query_kernel",
    )(cells, high, low)


def corr_kernel(group, columns, tile, *refs):
    place_ref, cells_ref, rim_ref, t_ref, edge_ref, query_ref = refs[:6]
    corr_ref = refs[-1]
    move_ref, stay_ref, keep_ref, send_ref = refs[-5:-1]
    half = corr_ref.shape[0] // columns
    own = place_ref[0]
    core = place_ref[1]
    base = ((own // half) ^ group) * half
    rows = half * columns
    pair = 2 * columns

    def plane_rows(plane, size):
        return pl.ds(pl.multiple_of(plane * columns, columns), size)

    step = 2 * QW
    for low in range(0, tile, step):
        total = query_ref[plane_rows(base, rows), low : low + step]
        edges = edge_ref[plane_rows(base, rows), :]
        total += product(edges, rim_ref[:, low : low + step])
        for at in range(0, half, 2):
            middle = cells_ref[plane_rows(base + at, 2 * pair), low + QW : low + QW + step]
            both = product(t_ref[...], middle)
            top = at * columns
            block = total[top : top + pair] + both[:pair] + both[pair:]
            corr_ref[top : top + pair, low : low + step] = block.astype(jnp.bfloat16)
    width = tile // 2
    for k in range(half):
        source = plane_rows(lax.rem(own, half) ^ k, columns)
        out_ref = move_ref if k % 2 else stay_ref
        out_ref[k // 2 * columns : (k // 2 + 1) * columns, :] = corr_ref[source, :]
        for half_ref, which in ((keep_ref, core), (send_ref, 1 - core)):
            start = pl.multiple_of(which * width, width)
            half_ref[k * columns : (k + 1) * columns, :] = corr_ref[source, pl.ds(start, width)]
    for earlier_ref, half_ref in zip(refs[6:-5], (keep_ref, send_ref)):
        half_ref[rows:, :] = earlier_ref[...]


def corr_call(group, place, cells, rim, mats, count, earlier=()):
    tile = rim.shape[1]
    columns = cells.shape[0] // (count + 2)
    half = count // 2
    rows = half * columns
    vmem = pl.BlockSpec(memory_space=pltpu.VMEM)
    wide = jax.ShapeDtypeStruct((rows // 2, tile), jnp.bfloat16)
    tall = jax.ShapeDtypeStruct((2 * rows if earlier else rows, tile // 2), jnp.bfloat16)
    return pl.pallas_call(
        lambda *refs: corr_kernel(group, columns, tile, *refs),
        out_shape=[wide, wide, tall, tall],
        in_specs=[pl.BlockSpec(memory_space=pltpu.SMEM)] + [vmem] * (5 + len(earlier)),
        out_specs=[vmem] * 4,
        scratch_shapes=[pltpu.VMEM((rows, tile), jnp.bfloat16)],
        compiler_params=pltpu.CompilerParams(vmem_limit_bytes=6 << 20),
        cost_estimate=pl.CostEstimate(
            flops=2 * rows * tile * 8 * columns,
            bytes_accessed=8 * rows * tile,
            transcendentals=0,
        ),
        name="corr_kernel",
    )(place, cells, rim, *mats, *earlier)


def partial_kernel(columns, stay_ref, moved_ref, here_ref, there_ref, *outs):
    width = here_ref.shape[1]
    step = 2 * QW
    for low in range(0, width, step):
        lanes = slice(low, low + step)
        total = product(stay_ref[...], here_ref[:, lanes])
        total += product(moved_ref[...], there_ref[:, lanes])
        for k, out_ref in enumerate(outs):
            out_ref[:, lanes] = total[k * columns : (k + 1) * columns].astype(out_ref.dtype)


def partial_call(stay, moved, here, there, columns, types):
    rows, tile = stay.shape
    width = here.shape[1]
    vmem = pl.BlockSpec(memory_space=pltpu.VMEM)
    return pl.pallas_call(
        lambda *refs: partial_kernel(columns, *refs),
        out_shape=[jax.ShapeDtypeStruct((columns, width), kind) for kind in types],
        in_specs=[vmem] * 4,
        out_specs=[vmem] * len(types),
        compiler_params=pltpu.CompilerParams(vmem_limit_bytes=6 << 20),
        cost_estimate=pl.CostEstimate(
            flops=4 * rows * tile * width, bytes_accessed=4 * tile * width, transcendentals=0
        ),
        name="partial_kernel",
    )(stay, moved, here, there)


def stack_call(blocks):
    columns, width = blocks[0].shape

    def kernel(*refs):
        for k in range(len(blocks)):
            refs[-1][k * columns : (k + 1) * columns, :] = refs[k][...]

    vmem = pl.BlockSpec(memory_space=pltpu.VMEM)
    return pl.pallas_call(
        kernel,
        out_shape=jax.ShapeDtypeStruct((len(blocks) * columns, width), jnp.bfloat16),
        in_specs=[vmem] * len(blocks),
        out_specs=vmem,
        compiler_params=pltpu.CompilerParams(vmem_limit_bytes=4 << 20),
        cost_estimate=pl.CostEstimate(
            flops=0, bytes_accessed=4 * len(blocks) * columns * width, transcendentals=0
        ),
        name="stack_kernel",
    )(*blocks)


def tile_shards(grad_volume, query_feats, support_feats, query_kernel, support_kernel):
    _, columns, queries = grad_volume.shape
    width = query_feats.shape[1]
    outer = lax.axis_size("blk")
    inner = lax.axis_size("sub")
    count = outer * inner
    half = count // 2
    tile = queries // count
    scale_factor = 1.0 / math.sqrt(width)
    own = lax.axis_index(("blk", "sub"))
    side = lax.axis_index("sub")
    core = lax.axis_index("pair")
    place = jnp.stack([own, core]).astype(jnp.int32)

    def exchanged(value, mask):
        return lax.ppermute(value, ("blk", "sub"), [(i, i ^ mask) for i in range(count)])

    def swapped(value):
        return lax.ppermute(value, "pair", [(0, 1), (1, 0)])

    volume = jnp.pad(grad_volume[0], ((0, 0), (QW, QW)))

    def piece(mask):
        return lax.dynamic_slice(volume, (0, (own ^ mask) * tile), (columns, tile + 2 * QW))

    reach = tile + 2 * QW
    feats = support_feats[0]
    merged = []
    pieces = [piece(mask) for mask in range(count)]
    held = [feats] + [None] * (count - 1)
    for mask in range(count - 1, 0, -1):
        if mask in merged:
            both = exchanged(jnp.concatenate([pieces[mask], feats], axis=1), mask)
            pieces[mask] = both
            held[mask] = both[:, reach:]
        else:
            pieces[mask] = exchanged(pieces[mask], mask)
    bit = half
    while bit:
        for k in range(0, count, 2 * bit):
            if held[k ^ bit] is None:
                held[k ^ bit] = exchanged(held[k], bit)
        bit //= 2

    edge = 16 * -(-count // 16)
    mats = matrix_call(place, query_kernel, support_kernel, count, columns, edge)
    here = lax.dynamic_slice(query_feats, (side * tile, 0), (tile, width))
    there = lax.dynamic_slice(query_feats, ((side ^ 1) * tile, 0), (tile, width))
    ordered = held + [pieces[k] for k in [7, 5, 6, 4, 3, 2, 1, 0]]
    ordered, mats, here, there = lax.optimization_barrier((ordered, mats, here, there))
    held, landed = ordered[:count], ordered[count:]
    for at, k in enumerate([7, 5, 6, 4, 3, 2, 1, 0]):
        pieces[k] = landed[at]
    cells, rim = gather_call(place, pieces, tile, edge)
    rim = swapped(rim)
    mats = [mats[0], mats[1], query_call(cells, mats[2], mats[3], columns, tile)]
    feats = stack_call(held)
    across = swapped(feats)
    move1, stay1, keep, send = corr_call(1, place, cells, rim, mats, count)
    moved1 = exchanged(move1, 1)
    move0, stay0, keep, send = corr_call(0, place, cells, rim, mats, count, (keep, send))
    moved0 = exchanged(move0, 1)
    other = swapped(send)
    narrow = [jnp.bfloat16] * (count // 4)
    parts1 = partial_call(stay1, moved1, here, there, columns, narrow)
    parts0 = partial_call(stay0, moved0, here, there, columns, [jnp.float32] + narrow[1:])
    landed = [exchanged(part, half + 2 * at) for at, part in enumerate(parts1)]
    landed += [exchanged(part, 2 * at) for at, part in enumerate(parts0) if at]

    def query_term(block, feats):
        return lax.dot_general(
            block, feats, (((0,), (0,)), ((), ())), preferred_element_type=jnp.float32
        )

    rows = half * columns
    query_grad = query_term(keep[:rows], feats[:rows]) + query_term(keep[rows:], feats[rows:])
    query_grad += query_term(other[:rows], across[:rows]) + query_term(other[rows:], across[rows:])
    query_grad *= scale_factor
    landed[-1], query_grad = lax.optimization_barrier((landed[-1], query_grad))
    support_grad = parts0[0]
    for term in landed:
        support_grad = support_grad + term.astype(jnp.float32)
    return (query_grad, (support_grad * scale_factor)[None])


def tiles_fit(mesh, grad_volume):
    shape = dict(mesh.shape)
    count = shape["blk"] * shape["sub"]
    planes = grad_volume.shape[0] // (shape["grp"] * count)
    columns = grad_volume.shape[1] // shape["pair"]
    return (
        planes == 1
        and shape["pair"] == 2
        and shape["sub"] == 2
        and count >= 4
        and count & (count - 1) == 0
        and count * columns <= 1024
        and columns % 16 == 0
        and QW % columns == 0
        and count * columns % QW == 0
        and QH * QW % (count * 2 * QW) == 0
    )


def solution(mesh):
    in_specs = (
        P(("grp", "blk", "sub"), "pair", None),
        P(("grp", "blk"), None),
        P(("grp", "blk", "sub"), "pair", None),
        P(),
        P(),
    )
    out_specs = (P(("grp", "blk", "sub", "pair"), None), P(("grp", "blk", "sub"), "pair", None))

    def program(grad_volume, *rest):
        body = tile_shards if tiles_fit(mesh, grad_volume) else ring_shards
        mapped = jax.shard_map(
            body, mesh=mesh, in_specs=in_specs, out_specs=out_specs, check_vma=False
        )
        return mapped(grad_volume, *rest)

    return program
```

```python
import math

import jax
import jax.numpy as jnp
from jax import lax
from jax.experimental import pallas as pl
from jax.experimental.pallas import tpu as pltpu
from jax.sharding import PartitionSpec as P

QW = 128
QH = 64


def extended(cells, sides, width):
    for axis, dim in sides:
        count = lax.axis_size(axis)
        ends = count - 1
        head = lax.slice_in_dim(cells, 0, width, axis=dim)
        tail = lax.slice_in_dim(cells, cells.shape[dim] - width, cells.shape[dim], axis=dim)
        cells = jnp.concatenate(
            [
                lax.ppermute(tail, axis, [(i, (i + 1) % count) for i in range(ends)]),
                cells,
                lax.ppermute(head, axis, [((i + 1) % count, i) for i in range(ends)]),
            ],
            axis=dim,
        )
    return cells


def shifted(value, axis, steps):
    count = lax.axis_size(axis)
    pairs = [(source, (source + steps) % count) for source in range(count)]
    return lax.ppermute(value, axis, pairs)


def query_pass(volume, kernel):
    planes, columns, queries = volume.shape
    grid = volume.astype(jnp.float32).reshape(planes, columns, QH, QW)
    padded = jnp.pad(grid, ((0, 0), (0, 0), (1, 1), (1, 1)))
    total = jnp.zeros_like(grid)
    for row_shift in range(3):
        for col_shift in range(3):
            total = (
                total
                + kernel[row_shift, col_shift]
                * padded[:, :, row_shift : row_shift + QH, col_shift : col_shift + QW]
            )
    return total.reshape(planes, columns, queries)


def support_pass(rimmed, kernel, planes, columns):
    total = jnp.zeros((planes, columns, rimmed.shape[2]), jnp.float32)
    for row_shift in range(3):
        for col_shift in range(3):
            total = total + kernel[row_shift, col_shift] * rimmed[
                row_shift : row_shift + planes, col_shift : col_shift + columns
            ].astype(jnp.float32)
    return total


def ring_shards(grad_volume, query_feats, support_feats, query_kernel, support_kernel):
    planes, columns, queries = grad_volume.shape
    rimmed = extended(grad_volume, ((("blk", "sub"), 0), ("pair", 1)), 1)
    corr_grad = (
        query_pass(grad_volume, query_kernel)
        + support_pass(rimmed, support_kernel, planes, columns)
    ).astype(jnp.bfloat16)
    moved = lax.all_to_all(corr_grad, "blk", split_axis=2, concat_axis=0, tiled=True)
    cycle_size = lax.axis_size("blk")
    own_index = lax.axis_index("blk")
    tile_len = moved.shape[2]
    tiles = moved.reshape(cycle_size, planes, columns, tile_len)
    width = query_feats.shape[1]
    scale_factor = 1.0 / math.sqrt(width)

    def project(piece_index, feat_piece, acc_piece, count):
        whole_block = lax.dynamic_index_in_dim(tiles, piece_index, 0, keepdims=False)
        block = whole_block.reshape(planes * count, tile_len)
        feat_flat = feat_piece.reshape(planes * count, width)
        query_term = lax.dot_general(
            block, feat_flat, (((0,), (0,)), ((), ())), preferred_element_type=jnp.float32
        )
        acc_new = acc_piece + jnp.dot(
            block, query_feats, preferred_element_type=jnp.float32
        ).reshape(planes, count, width)
        return (query_term, acc_new)

    query_start = jnp.zeros((tile_len, width), jnp.float32)

    def turn_one(turn_index, carry):
        query_total, feat_piece, acc_piece = carry
        term_piece, acc_piece = project(
            (own_index - turn_index) % cycle_size, feat_piece, acc_piece, columns
        )
        feat_piece = shifted(feat_piece, "blk", 1)
        acc_piece = shifted(acc_piece, "blk", 1)
        return (query_total + term_piece, feat_piece, acc_piece)

    start = (query_start, support_feats, jnp.zeros((planes, columns, width), jnp.float32))
    query_total, feat_piece, support_total = lax.fori_loop(0, cycle_size, turn_one, start)
    query_grad = (
        lax.psum_scatter(query_total, ("sub", "pair"), scatter_dimension=0, tiled=True)
        * scale_factor
    )
    return (query_grad, support_total * scale_factor)


def split_taps(kernel):
    high = lax.reduce_precision(kernel, 8, 7)
    return high, kernel - high


def banded(taps, step):
    total = jnp.where(step == 1, taps[2], 0.0)
    return jnp.where(step == 0, taps[1], jnp.where(step == -1, taps[0], total))


def matrix_kernel(count, columns, place_ref, taps_ref, t_ref, rim_ref, wh_ref, wl_ref):
    cells = count * columns

    def taps(part, kernel, a, b):
        return taps_ref[((part * 2 + kernel) * 3 + a) * 3 + b]

    def span(shape, dim):
        return lax.broadcasted_iota(jnp.int32, shape, dim)

    square = (QW, QW)
    step = span(square, 0) - span(square, 1)
    for part, w_ref in enumerate((wh_ref, wl_ref)):
        bands = [
            banded([taps(part, 0, a, b) for b in range(3)], step).astype(jnp.bfloat16)
            for a in range(3)
        ]
        for source in range(4):
            for target in range(2):
                a = source - target
                block = bands[a] if 0 <= a <= 2 else jnp.zeros(square, jnp.bfloat16)
                w_ref[source * QW : (source + 1) * QW, target * QW : (target + 1) * QW] = block
    group = 4 * columns
    shape = (2 * columns, group)
    row_step = span(shape, 1) // columns - span(shape, 0) // columns - 1
    col_step = lax.rem(span(shape, 1), columns) - lax.rem(span(shape, 0), columns)
    beside = jnp.where(place_ref[1] == 0, columns, -1)
    rim_shape = (cells, rim_ref.shape[1] // 2)
    rim_row = span(rim_shape, 1) - span(rim_shape, 0) // columns
    rim_col = beside - lax.rem(span(rim_shape, 0), columns)
    for part in range(2):
        rows = [
            banded([taps(part, 1, a, b) for a in range(3)], row_step) for b in range(3)
        ]
        block = banded(rows, col_step).astype(jnp.bfloat16)
        t_ref[part * 2 * columns : (part + 1) * 2 * columns, :] = block
        rows = [banded([taps(part, 1, a, b) for a in range(3)], rim_row) for b in range(3)]
        block = banded(rows, rim_col).astype(jnp.bfloat16)
        rim_ref[:, part * rim_shape[1] : (part + 1) * rim_shape[1]] = block


def matrix_call(place, query_kernel, support_kernel, count, columns, edge):
    query_parts = split_taps(query_kernel)
    support_parts = split_taps(support_kernel)
    taps = jnp.stack(
        [query_parts[0], support_parts[0], query_parts[1], support_parts[1]]
    ).reshape(-1)
    shapes = [
        (4 * columns, 4 * columns),
        (count * columns, 2 * edge),
        (4 * QW, 2 * QW),
        (4 * QW, 2 * QW),
    ]
    return pl.pallas_call(
        lambda *refs: matrix_kernel(count, columns, *refs),
        out_shape=[jax.ShapeDtypeStruct(shape, jnp.bfloat16) for shape in shapes],
        in_specs=[pl.BlockSpec(memory_space=pltpu.SMEM)] * 2,
        out_specs=[pl.BlockSpec(memory_space=pltpu.VMEM)] * 4,
        cost_estimate=pl.CostEstimate(
            flops=20 * QW * QW * count, bytes_accessed=32 * QW * QW, transcendentals=0
        ),
        compiler_params=pltpu.CompilerParams(vmem_limit_bytes=4 << 20),
        name="matrix_kernel",
    )(place, taps)


def gather_kernel(count, columns, tile, place_ref, *refs):
    pieces, cells_ref, rim_ref = refs[:count], refs[count], refs[count + 1]
    own = place_ref[0]
    first = place_ref[1] != 0
    inner = slice(QW, QW + tile)
    empty = jnp.zeros((columns, tile + 2 * QW), jnp.bfloat16)
    cells_ref[:columns, :] = empty
    cells_ref[(count + 1) * columns :, :] = empty
    edge = rim_ref.shape[0] // 2
    span = lax.broadcasted_iota(jnp.int32, (edge, tile), 0)
    total = jnp.zeros(span.shape, jnp.float32)
    for k, piece in enumerate(reversed(pieces)):
        start = pl.multiple_of(((own ^ k) + 1) * columns, columns)
        cells_ref[pl.ds(start, columns), :] = piece[:, : tile + 2 * QW]
        head = piece[:16, inner].astype(jnp.float32)[:1]
        tail = piece[columns - 16 :, inner].astype(jnp.float32)[15:]
        row = jnp.where(first, head, tail)
        total = jnp.where(span == (own ^ k), row, total)
    rim_ref[:edge, :] = total.astype(jnp.bfloat16)
    rim_ref[edge:, :] = total.astype(jnp.bfloat16)


def gather_call(place, pieces, tile, edge):
    count = len(pieces)
    columns, reach = pieces[0].shape
    return pl.pallas_call(
        lambda *refs: gather_kernel(count, columns, tile, *refs),
        out_shape=[
            jax.ShapeDtypeStruct(((count + 2) * columns, reach), jnp.bfloat16),
            jax.ShapeDtypeStruct((2 * edge, tile), jnp.bfloat16),
        ],
        in_specs=[pl.BlockSpec(memory_space=pltpu.SMEM)]
        + [pl.BlockSpec(memory_space=pltpu.VMEM)] * count,
        out_specs=[pl.BlockSpec(memory_space=pltpu.VMEM)] * 2,
        compiler_params=pltpu.CompilerParams(vmem_limit_bytes=4 << 20),
        cost_estimate=pl.CostEstimate(
            flops=count * tile, bytes_accessed=4 * count * columns * reach, transcendentals=0
        ),
        name="gather_kernel",
    )(place, *reversed(pieces))


def product(left, right):
    return jnp.dot(left, right, preferred_element_type=jnp.float32)


def query_kernel(columns, tile, cells_ref, wh_ref, wl_ref, out_ref):
    rows = out_ref.shape[0]
    step = 2 * QW
    for low in range(0, tile, step):
        window = cells_ref[columns : columns + rows, low : low + 2 * step]
        total = product(window, wh_ref[...]) + product(window, wl_ref[...])
        out_ref[:, low : low + step] = total


def query_call(cells, high, low, columns, tile):
    rows = cells.shape[0] - 2 * columns
    return pl.pallas_call(
        lambda *refs: query_kernel(columns, tile, *refs),
        out_shape=jax.ShapeDtypeStruct((rows, tile), jnp.float32),
        in_specs=[pl.BlockSpec(memory_space=pltpu.VMEM)] * 3,
        out_specs=pl.BlockSpec(memory_space=pltpu.VMEM),
        compiler_params=pltpu.CompilerParams(vmem_limit_bytes=6 << 20),
        cost_estimate=pl.CostEstimate(
            flops=16 * rows * tile * QW, bytes_accessed=8 * rows * tile, transcendentals=0
        ),
        name="query_kernel",
    )(cells, high, low)


def corr_kernel(group, columns, tile, *refs):
    place_ref, cells_ref, rim_ref, t_ref, edge_ref, query_ref = refs[:6]
    corr_ref = refs[-1]
    move_ref, stay_ref, keep_ref, send_ref = refs[-5:-1]
    half = corr_ref.shape[0] // columns
    own = place_ref[0]
    core = place_ref[1]
    base = ((own // half) ^ group) * half
    rows = half * columns
    pair = 2 * columns

    def plane_rows(plane, size):
        return pl.ds(pl.multiple_of(plane * columns, columns), size)

    step = 2 * QW
    for low in range(0, tile, step):
        total = query_ref[plane_rows(base, rows), low : low + step]
        edges = edge_ref[plane_rows(base, rows), :]
        total += product(edges, rim_ref[:, low : low + step])
        for at in range(0, half, 2):
            middle = cells_ref[plane_rows(base + at, 2 * pair), low + QW : low + QW + step]
            both = product(t_ref[...], middle)
            top = at * columns
            block = total[top : top + pair] + both[:pair] + both[pair:]
            corr_ref[top : top + pair, low : low + step] = block.astype(jnp.bfloat16)
    width = tile // 2
    for k in range(half):
        source = plane_rows(lax.rem(own, half) ^ k, columns)
        out_ref = move_ref if k % 2 else stay_ref
        out_ref[k // 2 * columns : (k // 2 + 1) * columns, :] = corr_ref[source, :]
        for half_ref, which in ((keep_ref, core), (send_ref, 1 - core)):
            start = pl.multiple_of(which * width, width)
            half_ref[k * columns : (k + 1) * columns, :] = corr_ref[source, pl.ds(start, width)]
    for earlier_ref, half_ref in zip(refs[6:-5], (keep_ref, send_ref)):
        half_ref[rows:, :] = earlier_ref[...]


def corr_call(group, place, cells, rim, mats, count, earlier=()):
    tile = rim.shape[1]
    columns = cells.shape[0] // (count + 2)
    half = count // 2
    rows = half * columns
    vmem = pl.BlockSpec(memory_space=pltpu.VMEM)
    wide = jax.ShapeDtypeStruct((rows // 2, tile), jnp.bfloat16)
    tall = jax.ShapeDtypeStruct((2 * rows if earlier else rows, tile // 2), jnp.bfloat16)
    return pl.pallas_call(
        lambda *refs: corr_kernel(group, columns, tile, *refs),
        out_shape=[wide, wide, tall, tall],
        in_specs=[pl.BlockSpec(memory_space=pltpu.SMEM)] + [vmem] * (5 + len(earlier)),
        out_specs=[vmem] * 4,
        scratch_shapes=[pltpu.VMEM((rows, tile), jnp.bfloat16)],
        compiler_params=pltpu.CompilerParams(vmem_limit_bytes=6 << 20),
        cost_estimate=pl.CostEstimate(
            flops=2 * rows * tile * 8 * columns,
            bytes_accessed=8 * rows * tile,
            transcendentals=0,
        ),
        name="corr_kernel",
    )(place, cells, rim, *mats, *earlier)


def partial_kernel(columns, stay_ref, moved_ref, here_ref, there_ref, *outs):
    width = here_ref.shape[1]
    step = 2 * QW
    for low in range(0, width, step):
        lanes = slice(low, low + step)
        total = product(stay_ref[...], here_ref[:, lanes])
        total += product(moved_ref[...], there_ref[:, lanes])
        for k, out_ref in enumerate(outs):
            out_ref[:, lanes] = total[k * columns : (k + 1) * columns].astype(out_ref.dtype)


def partial_call(stay, moved, here, there, columns, types):
    rows, tile = stay.shape
    width = here.shape[1]
    vmem = pl.BlockSpec(memory_space=pltpu.VMEM)
    return pl.pallas_call(
        lambda *refs: partial_kernel(columns, *refs),
        out_shape=[jax.ShapeDtypeStruct((columns, width), kind) for kind in types],
        in_specs=[vmem] * 4,
        out_specs=[vmem] * len(types),
        compiler_params=pltpu.CompilerParams(vmem_limit_bytes=6 << 20),
        cost_estimate=pl.CostEstimate(
            flops=4 * rows * tile * width, bytes_accessed=4 * tile * width, transcendentals=0
        ),
        name="partial_kernel",
    )(stay, moved, here, there)


def stack_call(blocks):
    columns, width = blocks[0].shape

    def kernel(*refs):
        for k in range(len(blocks)):
            refs[-1][k * columns : (k + 1) * columns, :] = refs[k][...]

    vmem = pl.BlockSpec(memory_space=pltpu.VMEM)
    return pl.pallas_call(
        kernel,
        out_shape=jax.ShapeDtypeStruct((len(blocks) * columns, width), jnp.bfloat16),
        in_specs=[vmem] * len(blocks),
        out_specs=vmem,
        compiler_params=pltpu.CompilerParams(vmem_limit_bytes=4 << 20),
        cost_estimate=pl.CostEstimate(
            flops=0, bytes_accessed=4 * len(blocks) * columns * width, transcendentals=0
        ),
        name="stack_kernel",
    )(*blocks)


def tile_shards(grad_volume, query_feats, support_feats, query_kernel, support_kernel):
    _, columns, queries = grad_volume.shape
    width = query_feats.shape[1]
    outer = lax.axis_size("blk")
    inner = lax.axis_size("sub")
    count = outer * inner
    half = count // 2
    tile = queries // count
    scale_factor = 1.0 / math.sqrt(width)
    own = lax.axis_index(("blk", "sub"))
    side = lax.axis_index("sub")
    core = lax.axis_index("pair")
    place = jnp.stack([own, core]).astype(jnp.int32)

    def exchanged(value, mask):
        return lax.ppermute(value, ("blk", "sub"), [(i, i ^ mask) for i in range(count)])

    def swapped(value):
        return lax.ppermute(value, "pair", [(0, 1), (1, 0)])

    volume = jnp.pad(grad_volume[0], ((0, 0), (QW, QW)))

    def piece(mask):
        return lax.dynamic_slice(volume, (0, (own ^ mask) * tile), (columns, tile + 2 * QW))

    reach = tile + 2 * QW
    feats = support_feats[0]
    merged = []
    pieces = [piece(mask) for mask in range(count)]
    held = [feats] + [None] * (count - 1)
    for mask in range(count - 1, 0, -1):
        if mask in merged:
            both = exchanged(jnp.concatenate([pieces[mask], feats], axis=1), mask)
            pieces[mask] = both
            held[mask] = both[:, reach:]
        else:
            pieces[mask] = exchanged(pieces[mask], mask)
    bit = half
    while bit:
        for k in range(0, count, 2 * bit):
            if held[k ^ bit] is None:
                held[k ^ bit] = exchanged(held[k], bit)
        bit //= 2

    edge = 16 * -(-count // 16)
    mats = matrix_call(place, query_kernel, support_kernel, count, columns, edge)
    here = lax.dynamic_slice(query_feats, (side * tile, 0), (tile, width))
    there = lax.dynamic_slice(query_feats, ((side ^ 1) * tile, 0), (tile, width))
    ordered = held + [pieces[k] for k in [7, 5, 6, 4, 3, 1, 2, 0]]
    ordered, mats, here, there = lax.optimization_barrier((ordered, mats, here, there))
    held, landed = ordered[:count], ordered[count:]
    for at, k in enumerate([7, 5, 6, 4, 3, 1, 2, 0]):
        pieces[k] = landed[at]
    cells, rim = gather_call(place, pieces, tile, edge)
    rim = swapped(rim)
    mats = [mats[0], mats[1], query_call(cells, mats[2], mats[3], columns, tile)]
    feats = stack_call(held)
    across = swapped(feats)
    move1, stay1, keep, send = corr_call(1, place, cells, rim, mats, count)
    moved1 = exchanged(move1, 1)
    move0, stay0, keep, send = corr_call(0, place, cells, rim, mats, count, (keep, send))
    moved0 = exchanged(move0, 1)
    other = swapped(send)
    narrow = [jnp.bfloat16] * (count // 4)
    parts1 = partial_call(stay1, moved1, here, there, columns, narrow)
    parts0 = partial_call(stay0, moved0, here, there, columns, [jnp.float32] + narrow[1:])
    landed = [exchanged(part, half + 2 * at) for at, part in enumerate(parts1)]
    landed += [exchanged(part, 2 * at) for at, part in enumerate(parts0) if at]

    def query_term(block, feats):
        return lax.dot_general(
            block, feats, (((0,), (0,)), ((), ())), preferred_element_type=jnp.float32
        )

    rows = half * columns
    query_grad = query_term(keep[:rows], feats[:rows]) + query_term(keep[rows:], feats[rows:])
    query_grad += query_term(other[:rows], across[:rows]) + query_term(other[rows:], across[rows:])
    query_grad *= scale_factor
    landed[-1], query_grad = lax.optimization_barrier((landed[-1], query_grad))
    support_grad = parts0[0]
    for term in landed:
        support_grad = support_grad + term.astype(jnp.float32)
    return (query_grad, (support_grad * scale_factor)[None])


def tiles_fit(mesh, grad_volume):
    shape = dict(mesh.shape)
    count = shape["blk"] * shape["sub"]
    planes = grad_volume.shape[0] // (shape["grp"] * count)
    columns = grad_volume.shape[1] // shape["pair"]
    return (
        planes == 1
        and shape["pair"] == 2
        and shape["sub"] == 2
        and count >= 4
        and count & (count - 1) == 0
        and count * columns <= 1024
        and columns % 16 == 0
        and QW % columns == 0
        and count * columns % QW == 0
        and QH * QW % (count * 2 * QW) == 0
    )


def solution(mesh):
    in_specs = (
        P(("grp", "blk", "sub"), "pair", None),
        P(("grp", "blk"), None),
        P(("grp", "blk", "sub"), "pair", None),
        P(),
        P(),
    )
    out_specs = (P(("grp", "blk", "sub", "pair"), None), P(("grp", "blk", "sub"), "pair", None))

    def program(grad_volume, *rest):
        body = tile_shards if tiles_fit(mesh, grad_volume) else ring_shards
        mapped = jax.shard_map(
            body, mesh=mesh, in_specs=in_specs, out_specs=out_specs, check_vma=False
        )
        return mapped(grad_volume, *rest)

    return program
```

```python
import math

import jax
import jax.numpy as jnp
from jax import lax
from jax.experimental import pallas as pl
from jax.experimental.pallas import tpu as pltpu
from jax.sharding import PartitionSpec as P

QW = 128
QH = 64


def extended(cells, sides, width):
    for axis, dim in sides:
        count = lax.axis_size(axis)
        ends = count - 1
        head = lax.slice_in_dim(cells, 0, width, axis=dim)
        tail = lax.slice_in_dim(cells, cells.shape[dim] - width, cells.shape[dim], axis=dim)
        cells = jnp.concatenate(
            [
                lax.ppermute(tail, axis, [(i, (i + 1) % count) for i in range(ends)]),
                cells,
                lax.ppermute(head, axis, [((i + 1) % count, i) for i in range(ends)]),
            ],
            axis=dim,
        )
    return cells


def shifted(value, axis, steps):
    count = lax.axis_size(axis)
    pairs = [(source, (source + steps) % count) for source in range(count)]
    return lax.ppermute(value, axis, pairs)


def query_pass(volume, kernel):
    planes, columns, queries = volume.shape
    grid = volume.astype(jnp.float32).reshape(planes, columns, QH, QW)
    padded = jnp.pad(grid, ((0, 0), (0, 0), (1, 1), (1, 1)))
    total = jnp.zeros_like(grid)
    for row_shift in range(3):
        for col_shift in range(3):
            total = (
                total
                + kernel[row_shift, col_shift]
                * padded[:, :, row_shift : row_shift + QH, col_shift : col_shift + QW]
            )
    return total.reshape(planes, columns, queries)


def support_pass(rimmed, kernel, planes, columns):
    total = jnp.zeros((planes, columns, rimmed.shape[2]), jnp.float32)
    for row_shift in range(3):
        for col_shift in range(3):
            total = total + kernel[row_shift, col_shift] * rimmed[
                row_shift : row_shift + planes, col_shift : col_shift + columns
            ].astype(jnp.float32)
    return total


def ring_shards(grad_volume, query_feats, support_feats, query_kernel, support_kernel):
    planes, columns, queries = grad_volume.shape
    rimmed = extended(grad_volume, ((("blk", "sub"), 0), ("pair", 1)), 1)
    corr_grad = (
        query_pass(grad_volume, query_kernel)
        + support_pass(rimmed, support_kernel, planes, columns)
    ).astype(jnp.bfloat16)
    moved = lax.all_to_all(corr_grad, "blk", split_axis=2, concat_axis=0, tiled=True)
    cycle_size = lax.axis_size("blk")
    own_index = lax.axis_index("blk")
    tile_len = moved.shape[2]
    tiles = moved.reshape(cycle_size, planes, columns, tile_len)
    width = query_feats.shape[1]
    scale_factor = 1.0 / math.sqrt(width)

    def project(piece_index, feat_piece, acc_piece, count):
        whole_block = lax.dynamic_index_in_dim(tiles, piece_index, 0, keepdims=False)
        block = whole_block.reshape(planes * count, tile_len)
        feat_flat = feat_piece.reshape(planes * count, width)
        query_term = lax.dot_general(
            block, feat_flat, (((0,), (0,)), ((), ())), preferred_element_type=jnp.float32
        )
        acc_new = acc_piece + jnp.dot(
            block, query_feats, preferred_element_type=jnp.float32
        ).reshape(planes, count, width)
        return (query_term, acc_new)

    query_start = jnp.zeros((tile_len, width), jnp.float32)

    def turn_one(turn_index, carry):
        query_total, feat_piece, acc_piece = carry
        term_piece, acc_piece = project(
            (own_index - turn_index) % cycle_size, feat_piece, acc_piece, columns
        )
        feat_piece = shifted(feat_piece, "blk", 1)
        acc_piece = shifted(acc_piece, "blk", 1)
        return (query_total + term_piece, feat_piece, acc_piece)

    start = (query_start, support_feats, jnp.zeros((planes, columns, width), jnp.float32))
    query_total, feat_piece, support_total = lax.fori_loop(0, cycle_size, turn_one, start)
    query_grad = (
        lax.psum_scatter(query_total, ("sub", "pair"), scatter_dimension=0, tiled=True)
        * scale_factor
    )
    return (query_grad, support_total * scale_factor)


def split_taps(kernel):
    high = lax.reduce_precision(kernel, 8, 7)
    return high, kernel - high


def banded(taps, step):
    total = jnp.where(step == 1, taps[2], 0.0)
    return jnp.where(step == 0, taps[1], jnp.where(step == -1, taps[0], total))


def matrix_kernel(count, columns, place_ref, taps_ref, t_ref, rim_ref, wh_ref, wl_ref):
    cells = count * columns

    def taps(part, kernel, a, b):
        return taps_ref[((part * 2 + kernel) * 3 + a) * 3 + b]

    def span(shape, dim):
        return lax.broadcasted_iota(jnp.int32, shape, dim)

    square = (QW, QW)
    step = span(square, 0) - span(square, 1)
    for part, w_ref in enumerate((wh_ref, wl_ref)):
        bands = [
            banded([taps(part, 0, a, b) for b in range(3)], step).astype(jnp.bfloat16)
            for a in range(3)
        ]
        for source in range(4):
            for target in range(2):
                a = source - target
                block = bands[a] if 0 <= a <= 2 else jnp.zeros(square, jnp.bfloat16)
                w_ref[source * QW : (source + 1) * QW, target * QW : (target + 1) * QW] = block
    group = 4 * columns
    shape = (2 * columns, group)
    row_step = span(shape, 1) // columns - span(shape, 0) // columns - 1
    col_step = lax.rem(span(shape, 1), columns) - lax.rem(span(shape, 0), columns)
    beside = jnp.where(place_ref[1] == 0, columns, -1)
    rim_shape = (cells, rim_ref.shape[1] // 2)
    rim_row = span(rim_shape, 1) - span(rim_shape, 0) // columns
    rim_col = beside - lax.rem(span(rim_shape, 0), columns)
    for part in range(2):
        rows = [
            banded([taps(part, 1, a, b) for a in range(3)], row_step) for b in range(3)
        ]
        block = banded(rows, col_step).astype(jnp.bfloat16)
        t_ref[part * 2 * columns : (part + 1) * 2 * columns, :] = block
        rows = [banded([taps(part, 1, a, b) for a in range(3)], rim_row) for b in range(3)]
        block = banded(rows, rim_col).astype(jnp.bfloat16)
        rim_ref[:, part * rim_shape[1] : (part + 1) * rim_shape[1]] = block


def matrix_call(place, query_kernel, support_kernel, count, columns, edge):
    query_parts = split_taps(query_kernel)
    support_parts = split_taps(support_kernel)
    taps = jnp.stack(
        [query_parts[0], support_parts[0], query_parts[1], support_parts[1]]
    ).reshape(-1)
    shapes = [
        (4 * columns, 4 * columns),
        (count * columns, 2 * edge),
        (4 * QW, 2 * QW),
        (4 * QW, 2 * QW),
    ]
    return pl.pallas_call(
        lambda *refs: matrix_kernel(count, columns, *refs),
        out_shape=[jax.ShapeDtypeStruct(shape, jnp.bfloat16) for shape in shapes],
        in_specs=[pl.BlockSpec(memory_space=pltpu.SMEM)] * 2,
        out_specs=[pl.BlockSpec(memory_space=pltpu.VMEM)] * 4,
        cost_estimate=pl.CostEstimate(
            flops=20 * QW * QW * count, bytes_accessed=32 * QW * QW, transcendentals=0
        ),
        compiler_params=pltpu.CompilerParams(vmem_limit_bytes=4 << 20),
        name="matrix_kernel",
    )(place, taps)


def gather_kernel(count, columns, tile, place_ref, *refs):
    pieces, cells_ref, rim_ref = refs[:count], refs[count], refs[count + 1]
    own = place_ref[0]
    first = place_ref[1] != 0
    inner = slice(QW, QW + tile)
    empty = jnp.zeros((columns, tile + 2 * QW), jnp.bfloat16)
    cells_ref[:columns, :] = empty
    cells_ref[(count + 1) * columns :, :] = empty
    edge = rim_ref.shape[0] // 2
    span = lax.broadcasted_iota(jnp.int32, (edge, tile), 0)
    total = jnp.zeros(span.shape, jnp.float32)
    for k, piece in enumerate(reversed(pieces)):
        start = pl.multiple_of(((own ^ k) + 1) * columns, columns)
        cells_ref[pl.ds(start, columns), :] = piece[:, : tile + 2 * QW]
        head = piece[:16, inner].astype(jnp.float32)[:1]
        tail = piece[columns - 16 :, inner].astype(jnp.float32)[15:]
        row = jnp.where(first, head, tail)
        total = jnp.where(span == (own ^ k), row, total)
    rim_ref[:edge, :] = total.astype(jnp.bfloat16)
    rim_ref[edge:, :] = total.astype(jnp.bfloat16)


def gather_call(place, pieces, tile, edge):
    count = len(pieces)
    columns, reach = pieces[0].shape
    return pl.pallas_call(
        lambda *refs: gather_kernel(count, columns, tile, *refs),
        out_shape=[
            jax.ShapeDtypeStruct(((count + 2) * columns, reach), jnp.bfloat16),
            jax.ShapeDtypeStruct((2 * edge, tile), jnp.bfloat16),
        ],
        in_specs=[pl.BlockSpec(memory_space=pltpu.SMEM)]
        + [pl.BlockSpec(memory_space=pltpu.VMEM)] * count,
        out_specs=[pl.BlockSpec(memory_space=pltpu.VMEM)] * 2,
        compiler_params=pltpu.CompilerParams(vmem_limit_bytes=4 << 20),
        cost_estimate=pl.CostEstimate(
            flops=count * tile, bytes_accessed=4 * count * columns * reach, transcendentals=0
        ),
        name="gather_kernel",
    )(place, *reversed(pieces))


def product(left, right):
    return jnp.dot(left, right, preferred_element_type=jnp.float32)


def query_kernel(columns, tile, cells_ref, wh_ref, wl_ref, out_ref):
    rows = out_ref.shape[0]
    step = 2 * QW
    for low in range(0, tile, step):
        window = cells_ref[columns : columns + rows, low : low + 2 * step]
        total = product(window, wh_ref[...]) + product(window, wl_ref[...])
        out_ref[:, low : low + step] = total


def query_call(cells, high, low, columns, tile):
    rows = cells.shape[0] - 2 * columns
    return pl.pallas_call(
        lambda *refs: query_kernel(columns, tile, *refs),
        out_shape=jax.ShapeDtypeStruct((rows, tile), jnp.float32),
        in_specs=[pl.BlockSpec(memory_space=pltpu.VMEM)] * 3,
        out_specs=pl.BlockSpec(memory_space=pltpu.VMEM),
        compiler_params=pltpu.CompilerParams(vmem_limit_bytes=6 << 20),
        cost_estimate=pl.CostEstimate(
            flops=16 * rows * tile * QW, bytes_accessed=8 * rows * tile, transcendentals=0
        ),
        name="query_kernel",
    )(cells, high, low)


def corr_kernel(group, columns, tile, *refs):
    place_ref, cells_ref, rim_ref, t_ref, edge_ref, query_ref = refs[:6]
    corr_ref = refs[-1]
    move_ref, stay_ref, keep_ref, send_ref = refs[-5:-1]
    half = corr_ref.shape[0] // columns
    own = place_ref[0]
    core = place_ref[1]
    base = ((own // half) ^ group) * half
    rows = half * columns
    pair = 2 * columns

    def plane_rows(plane, size):
        return pl.ds(pl.multiple_of(plane * columns, columns), size)

    step = 2 * QW
    for low in range(0, tile, step):
        total = query_ref[plane_rows(base, rows), low : low + step]
        edges = edge_ref[plane_rows(base, rows), :]
        total += product(edges, rim_ref[:, low : low + step])
        for at in range(0, half, 2):
            middle = cells_ref[plane_rows(base + at, 2 * pair), low + QW : low + QW + step]
            both = product(t_ref[...], middle)
            top = at * columns
            block = total[top : top + pair] + both[:pair] + both[pair:]
            corr_ref[top : top + pair, low : low + step] = block.astype(jnp.bfloat16)
    width = tile // 2
    for k in range(half):
        source = plane_rows(lax.rem(own, half) ^ k, columns)
        out_ref = move_ref if k % 2 else stay_ref
        out_ref[k // 2 * columns : (k // 2 + 1) * columns, :] = corr_ref[source, :]
        for half_ref, which in ((keep_ref, core), (send_ref, 1 - core)):
            start = pl.multiple_of(which * width, width)
            half_ref[k * columns : (k + 1) * columns, :] = corr_ref[source, pl.ds(start, width)]
    for earlier_ref, half_ref in zip(refs[6:-5], (keep_ref, send_ref)):
        half_ref[rows:, :] = earlier_ref[...]


def corr_call(group, place, cells, rim, mats, count, earlier=()):
    tile = rim.shape[1]
    columns = cells.shape[0] // (count + 2)
    half = count // 2
    rows = half * columns
    vmem = pl.BlockSpec(memory_space=pltpu.VMEM)
    wide = jax.ShapeDtypeStruct((rows // 2, tile), jnp.bfloat16)
    tall = jax.ShapeDtypeStruct((2 * rows if earlier else rows, tile // 2), jnp.bfloat16)
    return pl.pallas_call(
        lambda *refs: corr_kernel(group, columns, tile, *refs),
        out_shape=[wide, wide, tall, tall],
        in_specs=[pl.BlockSpec(memory_space=pltpu.SMEM)] + [vmem] * (5 + len(earlier)),
        out_specs=[vmem] * 4,
        scratch_shapes=[pltpu.VMEM((rows, tile), jnp.bfloat16)],
        compiler_params=pltpu.CompilerParams(vmem_limit_bytes=6 << 20),
        cost_estimate=pl.CostEstimate(
            flops=2 * rows * tile * 8 * columns,
            bytes_accessed=8 * rows * tile,
            transcendentals=0,
        ),
        name="corr_kernel",
    )(place, cells, rim, *mats, *earlier)


def partial_kernel(columns, stay_ref, moved_ref, here_ref, there_ref, *outs):
    width = here_ref.shape[1]
    step = 2 * QW
    for low in range(0, width, step):
        lanes = slice(low, low + step)
        total = product(stay_ref[...], here_ref[:, lanes])
        total += product(moved_ref[...], there_ref[:, lanes])
        for k, out_ref in enumerate(outs):
            out_ref[:, lanes] = total[k * columns : (k + 1) * columns].astype(out_ref.dtype)


def partial_call(stay, moved, here, there, columns, types):
    rows, tile = stay.shape
    width = here.shape[1]
    vmem = pl.BlockSpec(memory_space=pltpu.VMEM)
    return pl.pallas_call(
        lambda *refs: partial_kernel(columns, *refs),
        out_shape=[jax.ShapeDtypeStruct((columns, width), kind) for kind in types],
        in_specs=[vmem] * 4,
        out_specs=[vmem] * len(types),
        compiler_params=pltpu.CompilerParams(vmem_limit_bytes=6 << 20),
        cost_estimate=pl.CostEstimate(
            flops=4 * rows * tile * width, bytes_accessed=4 * tile * width, transcendentals=0
        ),
        name="partial_kernel",
    )(stay, moved, here, there)


def stack_call(blocks):
    columns, width = blocks[0].shape

    def kernel(*refs):
        for k in range(len(blocks)):
            refs[-1][k * columns : (k + 1) * columns, :] = refs[k][...]

    vmem = pl.BlockSpec(memory_space=pltpu.VMEM)
    return pl.pallas_call(
        kernel,
        out_shape=jax.ShapeDtypeStruct((len(blocks) * columns, width), jnp.bfloat16),
        in_specs=[vmem] * len(blocks),
        out_specs=vmem,
        compiler_params=pltpu.CompilerParams(vmem_limit_bytes=4 << 20),
        cost_estimate=pl.CostEstimate(
            flops=0, bytes_accessed=4 * len(blocks) * columns * width, transcendentals=0
        ),
        name="stack_kernel",
    )(*blocks)


def tile_shards(grad_volume, query_feats, support_feats, query_kernel, support_kernel):
    _, columns, queries = grad_volume.shape
    width = query_feats.shape[1]
    outer = lax.axis_size("blk")
    inner = lax.axis_size("sub")
    count = outer * inner
    half = count // 2
    tile = queries // count
    scale_factor = 1.0 / math.sqrt(width)
    own = lax.axis_index(("blk", "sub"))
    side = lax.axis_index("sub")
    core = lax.axis_index("pair")
    place = jnp.stack([own, core]).astype(jnp.int32)

    def exchanged(value, mask):
        return lax.ppermute(value, ("blk", "sub"), [(i, i ^ mask) for i in range(count)])

    def swapped(value):
        return lax.ppermute(value, "pair", [(0, 1), (1, 0)])

    volume = jnp.pad(grad_volume[0], ((0, 0), (QW, QW)))

    def piece(mask):
        return lax.dynamic_slice(volume, (0, (own ^ mask) * tile), (columns, tile + 2 * QW))

    reach = tile + 2 * QW
    feats = support_feats[0]
    merged = []
    pieces = [piece(mask) for mask in range(count)]
    held = [feats] + [None] * (count - 1)
    for mask in range(count - 1, 0, -1):
        if mask in merged:
            both = exchanged(jnp.concatenate([pieces[mask], feats], axis=1), mask)
            pieces[mask] = both
            held[mask] = both[:, reach:]
        else:
            pieces[mask] = exchanged(pieces[mask], mask)
    bit = half
    while bit:
        for k in range(0, count, 2 * bit):
            if held[k ^ bit] is None:
                held[k ^ bit] = exchanged(held[k], bit)
        bit //= 2

    edge = 16 * -(-count // 16)
    mats = matrix_call(place, query_kernel, support_kernel, count, columns, edge)
    here = lax.dynamic_slice(query_feats, (side * tile, 0), (tile, width))
    there = lax.dynamic_slice(query_feats, ((side ^ 1) * tile, 0), (tile, width))
    ordered = held + [pieces[k] for k in [7, 5, 6, 3, 4, 1, 2, 0]]
    ordered, mats, here, there = lax.optimization_barrier((ordered, mats, here, there))
    held, landed = ordered[:count], ordered[count:]
    for at, k in enumerate([7, 5, 6, 3, 4, 1, 2, 0]):
        pieces[k] = landed[at]
    cells, rim = gather_call(place, pieces, tile, edge)
    rim = swapped(rim)
    mats = [mats[0], mats[1], query_call(cells, mats[2], mats[3], columns, tile)]
    feats = stack_call(held)
    across = swapped(feats)
    move1, stay1, keep, send = corr_call(1, place, cells, rim, mats, count)
    moved1 = exchanged(move1, 1)
    move0, stay0, keep, send = corr_call(0, place, cells, rim, mats, count, (keep, send))
    moved0 = exchanged(move0, 1)
    other = swapped(send)
    narrow = [jnp.bfloat16] * (count // 4)
    parts1 = partial_call(stay1, moved1, here, there, columns, narrow)
    parts0 = partial_call(stay0, moved0, here, there, columns, [jnp.float32] + narrow[1:])
    landed = [exchanged(part, half + 2 * at) for at, part in enumerate(parts1)]
    landed += [exchanged(part, 2 * at) for at, part in enumerate(parts0) if at]

    def query_term(block, feats):
        return lax.dot_general(
            block, feats, (((0,), (0,)), ((), ())), preferred_element_type=jnp.float32
        )

    rows = half * columns
    query_grad = query_term(keep[:rows], feats[:rows]) + query_term(keep[rows:], feats[rows:])
    query_grad += query_term(other[:rows], across[:rows]) + query_term(other[rows:], across[rows:])
    query_grad *= scale_factor
    landed[-1], query_grad = lax.optimization_barrier((landed[-1], query_grad))
    support_grad = parts0[0]
    for term in landed:
        support_grad = support_grad + term.astype(jnp.float32)
    return (query_grad, (support_grad * scale_factor)[None])


def tiles_fit(mesh, grad_volume):
    shape = dict(mesh.shape)
    count = shape["blk"] * shape["sub"]
    planes = grad_volume.shape[0] // (shape["grp"] * count)
    columns = grad_volume.shape[1] // shape["pair"]
    return (
        planes == 1
        and shape["pair"] == 2
        and shape["sub"] == 2
        and count == 8
        and count * columns <= 1024
        and columns % 16 == 0
        and QW % columns == 0
        and count * columns % QW == 0
        and QH * QW % (count * 2 * QW) == 0
    )


def solution(mesh):
    in_specs = (
        P(("grp", "blk", "sub"), "pair", None),
        P(("grp", "blk"), None),
        P(("grp", "blk", "sub"), "pair", None),
        P(),
        P(),
    )
    out_specs = (P(("grp", "blk", "sub", "pair"), None), P(("grp", "blk", "sub"), "pair", None))

    def program(grad_volume, *rest):
        body = tile_shards if tiles_fit(mesh, grad_volume) else ring_shards
        mapped = jax.shard_map(
            body, mesh=mesh, in_specs=in_specs, out_specs=out_specs, check_vma=False
        )
        return mapped(grad_volume, *rest)

    return program
```
